32 devices in a mesh: row: 8 (over y, x, core), col: 4 (over z).
Axes of the slice: x: 2, y: 2, z: 4, core: 2. Of those that a mesh axis runs over, the one named last changes fastest.
Arguments:
- panel_tiles: float32 [16384, 1024], P('row', 'col'), may hold values from -48 to 48
- left_u: bfloat16 [16384, 6144], P('row', 'col'), may hold values from -8 to 8
- earlier_right_factors: bfloat16 [16384, 6144], P('row', 'col'), may hold values from -0.25 to 0.25
- tile_global_index: int32 [16], replicated, may hold values from 0 to 15, as said below
Outputs:
- panel_factor: float32 [16384, 1024], P('row', 'col')
The draws below stay inside these ranges and needn't reach their ends.
Inputs may be any that keep to these rules, and one draw needn't show every extreme that they name: `tile_global_index`: A permutation; slot pivot, the one numbered 0, holds the diagonal tile.
All inputs are finite; a program needn't handle non-finite values.
Results may differ from the reference program's by a relative error of at most 0.00053.
Values may be sent and summed in bfloat16 or wider, within the bound.
A program may use at most 128 MiB of HBM per device.

```python
import math
import jax
import jax.numpy as jnp
from jax import lax

TILE = 1024
RANK = 256
TILES = 16
COLS = 24


kernel_height = 30.0


nugget_level = 16.0


factor_bound = 0.25


def pivot_draw(key):
    ordering = jax.random.permutation(jax.random.fold_in(key, 11), TILES).astype(jnp.int32)
    pivot_position = jnp.sum(jnp.where(ordering == 0, jnp.arange(TILES, dtype=jnp.int32), 0)).astype(jnp.int32)
    return (ordering, pivot_position)


def update_scale():
    aspect_ratio = TILE / (COLS * RANK)
    edge_factor = (1.0 + math.sqrt(aspect_ratio)) ** 2 * (1.0 + 0.5 * RANK / TILE)
    margin_factor = 1.05 + 1.5 / math.sqrt(TILE)
    return math.sqrt(nugget_level / (edge_factor * margin_factor * COLS * RANK))


def draw_tile_global_index(key, part):
    ordering, pivot_position = pivot_draw(key)
    return ordering


def draw_panel_tiles(key, part):
    ordering, pivot_position = pivot_draw(key)
    background = jnp.clip(jax.random.normal(jax.random.fold_in(key, 21), (TILES * TILE, TILE), jnp.float32), -6.0, 6.0) * 0.5
    length_scale = 0.15
    points = jax.random.uniform(jax.random.fold_in(key, 24), (TILE, 2), jnp.float32)
    offsets = points[:, None, :] - points[None, :, :]
    distance = jnp.sqrt(jnp.sum(offsets * offsets, axis=2))
    pivot_block = kernel_height * jnp.exp(-distance / length_scale) + nugget_level * jnp.eye(TILE, dtype=jnp.float32)
    start_row = (pivot_position * TILE).astype(jnp.int32)
    result = lax.dynamic_update_slice(background, pivot_block, (start_row, jnp.int32(0)))
    return result.astype(jnp.float32)


def draw_left_u(key, part):
    ordering, pivot_position = pivot_draw(key)
    background = jnp.clip(jax.random.normal(jax.random.fold_in(key, 31), (TILES * TILE, COLS * RANK), jnp.float32), -6.0, 6.0) * 0.3
    pivot_rows = jnp.clip(jax.random.normal(jax.random.fold_in(key, 32), (TILE, COLS * RANK), jnp.float32), -6.0, 6.0) * update_scale()
    start_row = (pivot_position * TILE).astype(jnp.int32)
    result = lax.dynamic_update_slice(background, pivot_rows, (start_row, jnp.int32(0)))
    return result.astype(jnp.bfloat16)


def draw_earlier_right_factors(key, part):
    normal_draw = jnp.clip(jax.random.normal(jax.random.fold_in(key, 41), (TILES * TILE, COLS * RANK), jnp.float32), -6.0, 6.0)
    scaled = jnp.clip(normal_draw * (1.0 / math.sqrt(TILE)), -factor_bound, factor_bound)
    return scaled.astype(jnp.bfloat16)


def setup_inputs(seed: int = 0) -> dict:
    seeds = jax.random.split(jax.random.key(seed), 5)
    return {
        "panel_tiles": draw_panel_tiles(jax.random.fold_in(seeds[4], 71), 0),
        "left_u": draw_left_u(jax.random.fold_in(seeds[4], 71), 0),
        "earlier_right_factors": draw_earlier_right_factors(jax.random.fold_in(seeds[4], 71), 0),
        "tile_global_index": draw_tile_global_index(jax.random.fold_in(seeds[4], 71), 0),
    }


def reference(panel_tiles, left_u, earlier_right_factors, tile_global_index):
    pivot_position = jnp.sum(jnp.where(tile_global_index == 0, jnp.arange(TILES, dtype=jnp.int32), 0)).astype(jnp.int32)
    first_row = (pivot_position * TILE).astype(jnp.int32)
    pivot_left = lax.dynamic_slice_in_dim(left_u, first_row, TILE, 0)
    pivot_right = lax.dynamic_slice_in_dim(earlier_right_factors, first_row, TILE, 0)
    pivot_triple = pivot_right.astype(jnp.float32).reshape(TILE, COLS, RANK)

    def tile_update(factors):
        u_rows, v_rows = factors
        inner_small = jnp.einsum('bjr,bjs->jrs', v_rows.astype(jnp.float32).reshape(TILE, COLS, RANK), pivot_triple).astype(jnp.bfloat16)
        left_small = jnp.einsum('bjr,jrs->bjs', u_rows.astype(jnp.float32).reshape(TILE, COLS, RANK), inner_small.astype(jnp.float32)).astype(jnp.bfloat16)
        return jnp.dot(left_small.reshape(TILE, COLS * RANK).astype(jnp.float32), pivot_left.T.astype(jnp.float32), preferred_element_type=jnp.float32)
    update_terms = lax.map(tile_update, (left_u.reshape(TILES, TILE, COLS * RANK), earlier_right_factors.reshape(TILES, TILE, COLS * RANK)))
    updated_tiles = panel_tiles.reshape(TILES, TILE, TILE) - update_terms
    diagonal = lax.dynamic_index_in_dim(updated_tiles, pivot_position, 0, keepdims=False)
    cholesky_factor = jnp.linalg.cholesky(diagonal)
    identity = jnp.eye(TILE, dtype=jnp.float32)
    inverted_factor = lax.linalg.triangular_solve(cholesky_factor, identity, left_side=True, lower=True)
    solved_rows = jnp.einsum('fvk,ik->fvi', updated_tiles, inverted_factor, precision=lax.Precision.HIGHEST)
    chosen = (jnp.arange(TILES, dtype=jnp.int32) == pivot_position)[:, None, None]
    result = jnp.where(chosen, cholesky_factor[None, :, :], solved_rows)
    return result.reshape(TILES * TILE, TILE)
```

```python
import functools

import jax
import jax.numpy as jnp
from jax import lax
from jax.experimental import pallas as pl
from jax.experimental.pallas import tpu as pltpu
from jax.sharding import PartitionSpec as P

TILE = 1024
RANK = 256

BLK = 128
SUB = 8
F32 = jnp.float32
BF16 = jnp.bfloat16
HI = lax.Precision.HIGHEST
MESH = pl.DeviceIdType.MESH
ANY = pl.BlockSpec(memory_space=pl.ANY)
VM = pl.BlockSpec(memory_space=pltpu.VMEM)
TRANS = (((1,), (1,)), ((), ()))


def dot(a, b, dims=((1,), (0,))):
    return lax.dot_general(a, b, (dims, ((), ())), precision=HI, preferred_element_type=F32)


def window(start, size):
    return pl.ds(pl.multiple_of(start, size), size)


def remote(src, dst, send, recv, target):
    return pltpu.make_async_remote_copy(
        src_ref=src, dst_ref=dst, send_sem=send, recv_sem=recv, device_id=target, device_id_type=MESH
    )


def pick(table, index):
    value = jnp.int32(table[0])
    for i in range(1, len(table)):
        value = jnp.where(index == i, jnp.int32(table[i]), value)
    return value


def spread_kernel(
    owner, row_devices, pieces, v_mine, u_mine, a_mine, v_ref, u_ref, left_ref, pu_ref, part_ref,
    pv, v_own, u_own, pvt, a_got, sends, recvs, a_send, a_recv, local_sem,
):
    me = lax.axis_index("row")
    col = lax.axis_index("col")
    chips = row_devices // 2
    chip, core = me // 2, me % 2
    order = [i ^ (i >> 1) for i in range(chips)]
    if len(set(order)) != chips or max(order) >= chips:
        order = list(range(chips))
    place_of = [order.index(c) for c in range(chips)]
    home = place_of[owner // 2]
    place = pick(place_of, chip)
    forward = 1 - 2 * core
    hops = (chips + forward * (place - home)) % chips
    onward = pick(order, (place + chips + forward) % chips) * 2 + core
    pair = chip * 2 + 1 - core
    tile, width = pu_ref.shape
    half = tile // 2
    step = half // pieces
    share = tile // row_devices
    rank = RANK
    blocks = width // rank
    slots = v_ref.shape[0] // tile

    loads = [
        pltpu.make_async_copy(v_ref, v_own, local_sem.at[0]),
        pltpu.make_async_copy(u_ref, u_own, local_sem.at[1]),
    ]
    for item in loads:
        item.start()

    barrier = pltpu.get_barrier_semaphore()
    for d in range(1, row_devices):
        pl.semaphore_signal(barrier, inc=1, device_id=((me + d) % row_devices, col), device_id_type=MESH)
    pl.semaphore_wait(barrier, row_devices - 1)

    def rows(stream, i):
        return window(stream * half + i * step, step)

    def hop(kind, stream, i, target, src=None):
        dst = (pv, pu_ref)[kind].at[rows(stream, i), :]
        return remote(
            dst if src is None else src.at[rows(stream, i), :], dst,
            sends.at[kind, stream, i], recvs.at[kind, stream, i], target,
        )

    def cross(kind, stream, i, target, src=None):
        dst = (pv, pu_ref)[kind].at[rows(stream, i), :]
        return remote(
            dst if src is None else src.at[rows(stream, i), :], dst,
            sends.at[2 + kind, stream, i], recvs.at[kind, stream, i], target,
        )

    is_owner = me == owner
    away = chip != owner // 2
    last = hops == chips - 1
    to_right = order[(home + 1) % chips] * 2
    to_left = order[(home + chips - 1) % chips] * 2 + 1
    mine = [v_mine, u_mine]
    own_copy = [
        pltpu.make_async_copy(v_mine, pv, local_sem.at[2]),
        pltpu.make_async_copy(u_mine, pu_ref, local_sem.at[3]),
        pltpu.make_async_copy(a_mine.at[window(owner * share, share), :], a_got, local_sem.at[4]),
    ]

    def a_piece(target):
        return remote(a_mine.at[window(target * share, share), :], a_got, a_send.at[target], a_recv, (target, col))

    @pl.when(is_owner)
    def _():
        for kind in range(2):

            @pl.loop(0, pieces)
            def _(i):
                hop(kind, 0, i, (to_right, col), mine[kind]).start()
                hop(kind, 1, i, (to_left, col), mine[kind]).start()
                cross(kind, 0, i, (pair, col), mine[kind]).start()
                cross(kind, 1, i, (pair, col), mine[kind]).start()

            if kind == 0:
                for other in range(row_devices):
                    if other != owner:
                        a_piece(other).start()
        for item in own_copy:
            item.start()

    def relay(kind, i):
        @pl.when(away)
        def _():
            hop(kind, core, i, (onward, col)).wait_recv()

            @pl.when(jnp.logical_not(last))
            def _():
                hop(kind, core, i, (onward, col)).start()

            cross(kind, core, i, (pair, col)).start()

    def gather(kind):
        @pl.when(jnp.logical_not(is_owner))
        def _():
            @pl.loop(0, pieces)
            def _(i):
                cross(kind, 1 - core, i, (pair, col)).wait_recv()

            @pl.when(jnp.logical_not(away))
            def _():
                @pl.loop(0, pieces)
                def _(i):
                    cross(kind, core, i, (pair, col)).wait_recv()

    @pl.loop(0, pieces)
    def _(i):
        relay(0, i)

    gather(0)

    @pl.when(is_owner)
    def _():
        own_copy[0].wait()

    for item in loads:
        item.wait()

    total = blocks * slots
    for b in range(blocks):
        at = slice(b * rank, (b + 1) * rank)
        pvt[at, :] = pv[:, at].T
        for t in range(slots):
            here = slice(t * tile, (t + 1) * tile)
            inner = jnp.dot(pvt[at, :], v_own[here, at], preferred_element_type=F32).astype(BF16)
            left_ref[here, at] = lax.dot_general(
                u_own[here, at], inner, TRANS, preferred_element_type=F32
            ).astype(BF16)
            done = b * slots + t
            for i in range(done * pieces // total, (done + 1) * pieces // total):
                relay(1, i)

    gather(1)

    @pl.when(is_owner)
    def _():
        own_copy[1].wait()
        own_copy[2].wait()

    @pl.when(jnp.logical_not(is_owner))
    def _():
        a_piece(owner).wait_recv()

    small = []
    for b in range(blocks):
        at = slice(b * rank, (b + 1) * rank)
        inner = jnp.dot(pvt[at, :], pv[:, at], preferred_element_type=F32).astype(BF16)
        small.append(
            lax.dot_general(
                pu_ref[window(me * share, share), at], inner, TRANS, preferred_element_type=F32
            ).astype(BF16)
        )
    small = jnp.concatenate(small, axis=1)
    part_ref[...] = -lax.dot_general(small, pu_ref[...], TRANS, preferred_element_type=F32)
    width_out = a_got.shape[1]
    mine_cols = window(col * width_out, width_out)
    part_ref[:, mine_cols] = part_ref[:, mine_cols] + a_got[...]

    @pl.when(is_owner)
    def _():
        for kind in range(2):

            @pl.loop(0, pieces)
            def _(i):
                hop(kind, 0, i, (to_right, col), mine[kind]).wait_send()
                hop(kind, 1, i, (to_left, col), mine[kind]).wait_send()
                cross(kind, 0, i, (pair, col), mine[kind]).wait_send()
                cross(kind, 1, i, (pair, col), mine[kind]).wait_send()

        for other in range(row_devices):
            if other != owner:
                a_piece(other).wait_send()

    @pl.when(away)
    def _():
        for kind in range(2):

            @pl.loop(0, pieces)
            def _(i):
                @pl.when(jnp.logical_not(last))
                def _():
                    hop(kind, core, i, (onward, col)).wait_send()

                cross(kind, core, i, (pair, col)).wait_send()


def spread(mesh, owner, v_mine, u_mine, a_mine, v, u):
    row_devices = mesh.shape["row"]
    tile, width = v_mine.shape
    pieces = 8
    share = tile // row_devices
    return pl.pallas_call(
        functools.partial(spread_kernel, owner, row_devices, pieces),
        out_shape=(
            jax.ShapeDtypeStruct(u.shape, BF16),
            jax.ShapeDtypeStruct((tile, width), BF16),
            jax.ShapeDtypeStruct((share, tile), F32),
        ),
        in_specs=[VM, VM, VM, ANY, ANY],
        out_specs=(VM, VM, VM),
        scratch_shapes=[
            pltpu.VMEM((tile, width), BF16),
            pltpu.VMEM(v.shape, BF16),
            pltpu.VMEM(u.shape, BF16),
            pltpu.VMEM((width, tile), BF16),
            pltpu.VMEM((share, a_mine.shape[1]), F32),
            pltpu.SemaphoreType.DMA((4, 2, pieces)),
            pltpu.SemaphoreType.DMA((2, 2, pieces)),
            pltpu.SemaphoreType.DMA((row_devices,)),
            pltpu.SemaphoreType.DMA,
            pltpu.SemaphoreType.DMA((5,)),
        ],
        compiler_params=pltpu.CompilerParams(
            collective_id=1 + owner, has_side_effects=True, vmem_limit_bytes=48 * 1024 * 1024
        ),
        cost_estimate=pl.CostEstimate(flops=20_000_000_000, bytes_accessed=30_000_000, transcendentals=0),
        name="spread",
    )(v_mine, u_mine, a_mine, v, u)


def eliminate(block):
    shape = (SUB, BLK)
    groups = [block[g * SUB:(g + 1) * SUB, :] for g in range(BLK // SUB)]
    lane = lax.broadcasted_iota(jnp.int32, shape, 1)
    sub = lax.broadcasted_iota(jnp.int32, shape, 0)
    for g in range(len(groups)):
        base = g * SUB
        rows = groups[g]
        cols = [jnp.broadcast_to(rows[:, base + j:base + j + 1], shape) for j in range(SUB)]
        out = rows
        for s in range(SUB):
            raw = jnp.broadcast_to(rows[s:s + 1, :], shape)
            here = lane == base + s
            mine = sub == s
            out = jnp.where(mine, raw, out)
            inverse = 1.0 / jnp.broadcast_to(cols[s][s:s + 1, :], shape)
            factor = jnp.where(mine, 0.0, cols[s] * inverse)
            unit = jnp.where(here, 1.0, raw)
            kept = jnp.where(here, 0.0, rows)
            rows = jnp.where(mine, unit * inverse, kept - factor * unit)
            for j in range(s + 1, SUB):
                head = jnp.broadcast_to(cols[j][s:s + 1, :], shape)
                cols[j] = jnp.where(mine, head * inverse, cols[j] - factor * head)
        groups[g] = out
        if g + 1 == len(groups):
            break
        reduced = [jnp.broadcast_to(rows[s:s + 1, :], shape) for s in range(SUB)]
        inside = jnp.logical_and(lane >= base, lane < base + SUB)
        for h in range(g + 1, len(groups)):
            old = groups[h]
            terms = [
                jnp.broadcast_to(old[:, base + s:base + s + 1], shape) * reduced[s] for s in range(SUB)
            ]
            while len(terms) > 1:
                terms = [terms[i] + terms[i + 1] for i in range(0, len(terms), 2)]
            groups[h] = jnp.where(inside, 0.0, old) - terms[0]
    return jnp.concatenate(groups, axis=0)


def factor_step(k, w_ref, l_ref, x_ref):
    size = w_ref.shape[0]
    count = size // BLK
    row_id = lax.broadcasted_iota(jnp.int32, (BLK, BLK), 0)
    col_id = lax.broadcasted_iota(jnp.int32, (BLK, BLK), 1)
    at = window(k * BLK, BLK)
    done = eliminate(w_ref[at, at])
    pivots = jnp.sum(jnp.where(row_id == col_id, done, 0.0), axis=1, keepdims=True)
    scale = 1.0 / jnp.sqrt(pivots)
    upper = jnp.where(col_id >= row_id, done * scale, 0.0)
    inner = jnp.where(col_id < row_id, done * scale, 0.0) + jnp.where(row_id == col_id, scale, 0.0)
    l_ref[at, at] = upper.T
    row = dot(inner, w_ref[at, :])
    block_id = lax.broadcasted_iota(jnp.int32, (BLK, size), 1) // BLK
    row = jnp.where(block_id == k, jnp.concatenate([inner] * count, axis=1), row)
    x_ref[at, :] = jnp.where(block_id <= k, row, 0.0)
    inner_t = inner.T

    @pl.loop(k + 1, count)
    def _(i):
        there = window(i * BLK, BLK)
        left = dot(w_ref[there, at], inner_t)
        l_ref[there, at] = left
        w_ref[there, at] = jnp.zeros((BLK, BLK), F32)
        w_ref[there, :] = w_ref[there, :] - dot(left, row)


def panel_kernel(
    depth, row_devices, pieces, chunks, part_ref, left_ref, u_ref, a_ref, out_ref, lcol_ref,
    w_ref, l_ref, x_ref, acc, come, got,
    sends, recvs, pair_send, pair_recv, line_send, line_recv, out_send, out_recv,
):
    me = lax.axis_index("row")
    col = lax.axis_index("col")
    chips = row_devices // 2
    chip, core = me // 2, me % 2
    share = part_ref.shape[0]
    sub = share // depth
    pair = chip * 2 + 1 - core
    cols = [(col + d) % depth for d in range(1, depth)]
    peers = [((chip + d) % chips) * 2 + core for d in range(1, chips)]
    size = w_ref.shape[0]
    width = a_ref.shape[1]
    half = acc.shape[0] // 2
    piece = half // pieces
    count = size // BLK

    barrier = pltpu.get_barrier_semaphore()
    for other in cols:
        pl.semaphore_signal(barrier, inc=1, device_id=(me, other), device_id_type=MESH)
    for other in peers + [pair]:
        pl.semaphore_signal(barrier, inc=1, device_id=(other, col), device_id_type=MESH)
    pl.semaphore_wait(barrier, depth + chips - 1)

    first = []
    for d, other in enumerate(cols):
        first.append(
            remote(part_ref.at[window(other * sub, sub), :], got.at[d], sends.at[d], recvs.at[d], (me, other))
        )
        first[-1].start()

    mine_cols = window(col * width, width)

    def fill(lo, hi):
        @pl.loop(lo, hi)
        def _(i):
            at = window(i * 256, 256)
            acc[at, :] = -lax.dot_general(left_ref[at, :], u_ref[...], TRANS, preferred_element_type=F32)
            acc[at, mine_cols] = acc[at, mine_cols] + a_ref[at, :]

    strips = acc.shape[0] // 256
    fill(0, strips // 4)

    total = part_ref[window(col * sub, sub), :]
    for d, item in enumerate(first):
        item.wait_recv()
        total = total + got[d]
    mine = window(me * share + col * sub, sub)
    w_ref[mine, :] = total

    second = []
    for d, other in enumerate(cols):
        n = depth - 1 + d
        second.append(remote(w_ref.at[mine, :], w_ref.at[mine, :], sends.at[n], recvs.at[n], (me, other)))
        second[-1].start()
    fill(strips // 4, strips // 2)
    for item in second:
        item.wait_recv()

    block = w_ref.at[window(me * share, share), :]
    third = []
    for d, other in enumerate(peers):
        n = 2 * (depth - 1) + d
        third.append(remote(block, block, sends.at[n], recvs.at[n], (other, col)))
        third[-1].start()
    fill(strips // 2, strips)
    fourth = []
    for d in range(chips):
        if d:
            third[d - 1].wait_recv()
        holder = ((chip + chips - d) % chips) * 2 + core
        held = w_ref.at[window(holder * share, share), :]
        fourth.append(remote(held, held, pair_send.at[d], pair_recv.at[d], (pair, col)))
        fourth[-1].start()

    def line(way, i, target):
        at = window(way * half + i * piece, piece)
        return remote(acc.at[at, :], come.at[at, :], line_send.at[way, i], line_recv.at[way, i], (me, target))

    def pass_on(way, i, seat, target):
        @pl.when(jnp.logical_and(i >= 0, i < pieces))
        def _():
            at = window(way * half + i * piece, piece)

            @pl.when(seat > 0)
            def _():
                line(way, i, target).wait_recv()
                acc[at, :] = acc[at, :] + come[at, :]

            @pl.when(seat < depth - 1)
            def _():
                line(way, i, target).start()

    up = jnp.minimum(col + 1, depth - 1)
    down = jnp.maximum(col - 1, 0)
    seat_down = depth - 1 - col

    def line_step(tick):
        pass_on(0, tick - seat_down, seat_down, down)
        pass_on(1, tick - col, col, up)

    line_step(0)
    for item in fourth:
        item.wait_recv()
    for item in first + second + third + fourth:
        item.wait_send()

    @pl.loop(0, count)
    def _(i):
        at = window(i * BLK, BLK)
        l_ref[at, :] = jnp.zeros((BLK, size), F32)
        w_ref[at, at] = (w_ref[at, at] + w_ref[at, at].T) * 0.5

        @pl.loop(i + 1, count)
        def _(j):
            there = window(j * BLK, BLK)
            even = (w_ref[at, there] + w_ref[there, at].T) * 0.5
            w_ref[at, there] = even
            w_ref[there, at] = even.T

    ticks = pieces + depth - 1
    per = max(1, (ticks - 1) // count)

    @pl.loop(0, count)
    def _(k):
        @pl.loop(0, per)
        def _(s):
            line_step(1 + k * per + s)

        factor_step(k, w_ref, l_ref, x_ref)

    @pl.loop(1 + count * per, ticks)
    def _(tick):
        line_step(tick)

    lcol_ref[...] = l_ref[:, mine_cols]

    chunk = half // chunks

    def deal(way, i, c):
        at = window(way * half + i * chunk, chunk)
        return remote(
            come.at[at, c * width:(c + 1) * width], out_ref.at[at, :],
            out_send.at[i, c], out_recv.at[way, i], (me, c),
        )

    ends = [(0, 0), (1, depth - 1)]
    for way, end in ends:

        @pl.when(col == end)
        def _():
            @pl.loop(0, chunks)
            def _(i):
                at = window(way * half + i * chunk, chunk)
                for c in sorted(range(depth), key=lambda c: -abs(c - end)):
                    upto = (c + 1) * width
                    value = dot(acc[at, :upto], x_ref[c * width:upto, :upto], ((1,), (1,)))
                    if c == end:
                        out_ref[at, :] = value
                    else:
                        come[at, c * width:upto] = value
                        deal(way, i, c).start()

    for way, end in ends:

        @pl.when(col != end)
        def _():
            @pl.loop(0, chunks)
            def _(i):
                deal(way, i, 0).wait_recv()

    for way, end in ends:

        @pl.when(col == end)
        def _():
            @pl.loop(0, chunks)
            def _(i):
                for c in range(depth):
                    if c != end:
                        deal(way, i, c).wait_send()

    @pl.when(col > 0)
    def _():
        @pl.loop(0, pieces)
        def _(i):
            line(0, i, down).wait_send()

    @pl.when(col < depth - 1)
    def _():
        @pl.loop(0, pieces)
        def _(i):
            line(1, i, up).wait_send()


def panel(mesh, part, left, pivot_u, tiles):
    row_devices, depth = mesh.shape["row"], mesh.shape["col"]
    chips = row_devices // 2
    share, size = part.shape
    rows, width = tiles.shape
    pieces = rows // 2 // 64
    chunks = rows // 2 // 128
    links = 2 * (depth - 1) + chips - 1
    return pl.pallas_call(
        functools.partial(panel_kernel, depth, row_devices, pieces, chunks),
        out_shape=(
            jax.ShapeDtypeStruct((rows, width), F32),
            jax.ShapeDtypeStruct((size, width), F32),
        ),
        in_specs=[VM] * 4,
        out_specs=(VM, VM),
        scratch_shapes=[
            pltpu.VMEM((size, size), F32),
            pltpu.VMEM((size, size), F32),
            pltpu.VMEM((size, size), F32),
            pltpu.VMEM((rows, size), F32),
            pltpu.VMEM((rows, size), F32),
            pltpu.VMEM((depth - 1, share // depth, size), F32),
            pltpu.SemaphoreType.DMA((links,)),
            pltpu.SemaphoreType.DMA((links,)),
            pltpu.SemaphoreType.DMA((chips,)),
            pltpu.SemaphoreType.DMA((chips,)),
            pltpu.SemaphoreType.DMA((2, pieces)),
            pltpu.SemaphoreType.DMA((2, pieces)),
            pltpu.SemaphoreType.DMA((chunks, depth)),
            pltpu.SemaphoreType.DMA((2, chunks)),
        ],
        compiler_params=pltpu.CompilerParams(
            collective_id=0, has_side_effects=True, vmem_limit_bytes=58 * 1024 * 1024
        ),
        cost_estimate=pl.CostEstimate(flops=60_000_000_000, bytes_accessed=30_000_000, transcendentals=0),
        name="panel",
    )(part, left, pivot_u, tiles)


def local(mesh, panel_tiles, left_u, earlier_right_factors, tile_global_index):
    row_devices = mesh.shape["row"]
    tile_count = tile_global_index.shape[0]
    slots = panel_tiles.shape[0] // TILE
    pivot_position = jnp.sum(
        jnp.where(tile_global_index == 0, jnp.arange(tile_count, dtype=jnp.int32), 0)
    )
    owner_row = pivot_position // slots
    local_slot = pivot_position % slots

    def slot(value):
        return lax.dynamic_slice_in_dim(value, local_slot * TILE, TILE, 0)

    branches = [functools.partial(spread, mesh, owner) for owner in range(row_devices)]
    left, pivot_u, part = lax.switch(
        owner_row, branches,
        slot(earlier_right_factors), slot(left_u), slot(panel_tiles), earlier_right_factors, left_u,
    )
    solved, chol = panel(mesh, part, left, pivot_u, panel_tiles)
    chosen = jnp.logical_and(lax.axis_index("row") == owner_row, jnp.arange(slots) == local_slot)
    solved = solved.reshape(slots, TILE, -1)
    return jnp.where(chosen[:, None, None], chol[None], solved).reshape(panel_tiles.shape)


def solution(mesh):
    in_specs = (P("row", "col"), P("row", "col"), P("row", "col"), P())
    return jax.shard_map(
        functools.partial(local, mesh), mesh=mesh, in_specs=in_specs, out_specs=P("row", "col"), check_vma=False
    )
```

```python
import functools

import jax
import jax.numpy as jnp
from jax import lax
from jax.experimental import pallas as pl
from jax.experimental.pallas import tpu as pltpu
from jax.sharding import PartitionSpec as P

TILE = 1024
RANK = 256

BLK = 128
SUB = 8
FILL = 256
STRIP = 256
GROUP = 256
SKEW = 3
F32 = jnp.float32
BF16 = jnp.bfloat16
HI = lax.Precision.HIGHEST
MESH = pl.DeviceIdType.MESH
ANY = pl.BlockSpec(memory_space=pl.ANY)
VM = pl.BlockSpec(memory_space=pltpu.VMEM)
TRANS = (((1,), (1,)), ((), ()))


def dot(a, b, dims=((1,), (0,))):
    return lax.dot_general(a, b, (dims, ((), ())), precision=HI, preferred_element_type=F32)


def window(start, size):
    return pl.ds(pl.multiple_of(start, size), size)


def remote(src, dst, send, recv, target):
    return pltpu.make_async_remote_copy(
        src_ref=src, dst_ref=dst, send_sem=send, recv_sem=recv, device_id=target, device_id_type=MESH
    )


def pick(table, index):
    value = jnp.int32(table[0])
    for i in range(1, len(table)):
        value = jnp.where(index == i, jnp.int32(table[i]), value)
    return value


def spread_kernel(
    owner, row_devices, pieces, mask_ref, v_ref, u_ref, a_ref, left_ref, pu_ref, part_ref,
    pv, v_own, u_own, a_own, pvt, pin, a_mine, a_got, sends, recvs, a_send, a_recv, local_sem,
):
    me = lax.axis_index("row")
    col = lax.axis_index("col")
    chips = row_devices // 2
    chip, core = me // 2, me % 2
    order = [i ^ (i >> 1) for i in range(chips)]
    if max(order) >= chips:
        order = list(range(chips))
    home = order.index(owner // 2)
    home_core = owner % 2
    place = pick([order.index(c) for c in range(chips)], chip)
    nexts = [pick(order, (place + chips + w) % chips) * 2 + core for w in (1, -1)]
    hops = [(chips + w * (place - home)) % chips for w in (1, -1)]
    pair = chip * 2 + 1 - core
    tile, width = pu_ref.shape
    half = tile // 2
    step = half // (2 * pieces)
    share = tile // row_devices
    rank = RANK
    blocks = width // rank
    slots = v_ref.shape[0] // tile

    loads = [
        pltpu.make_async_copy(src, dst, local_sem.at[i])
        for i, (src, dst) in enumerate(((v_ref, v_own), (u_ref, u_own), (a_ref, a_own)))
    ]
    loads[0].start()

    barrier = pltpu.get_barrier_semaphore()
    for d in range(1, row_devices):
        pl.semaphore_signal(barrier, inc=1, device_id=((me + d) % row_devices, col), device_id_type=MESH)
    pl.semaphore_wait(barrier, row_devices - 1)
    loads[0].wait()
    loads[1].start()
    loads[2].start()

    bufs = (pv, pu_ref)

    def move(kind, way, side, i, target, lane):
        at = window(way * half + (2 * i + side) * step, step)
        ref = bufs[kind].at[at, :]
        return remote(ref, ref, sends.at[kind, lane, way, i], recvs.at[kind, way, side, i], (target, col))

    is_owner = me == owner
    away = chip != owner // 2
    helper = jnp.logical_and(jnp.logical_not(away), jnp.logical_not(is_owner))

    def a_piece(target):
        return remote(a_mine.at[window(target * share, share), :], a_got, a_send.at[target], a_recv, (target, col))

    def chosen(src, dst):
        @pl.loop(0, tile // BLK)
        def _(n):
            total = None
            for t in range(slots):
                keep = mask_ref[t:t + 1, :dst.shape[1]].astype(dst.dtype)
                term = src[window(t * tile + n * BLK, BLK), :] * keep
                total = term if total is None else total + term
            dst[window(n * BLK, BLK), :] = total

    def first_sends(kind):
        @pl.loop(0, pieces)
        def _(i):
            for way in range(2):
                move(kind, way, 1 - home_core, i, owner ^ 1, 2).start()
                move(kind, way, home_core, i, nexts[way], 0).start()
            for way in range(2):
                move(kind, way, home_core, i, owner ^ 1, 1).start()

    @pl.when(is_owner)
    def _():
        chosen(v_own, pv)
        first_sends(0)
        loads[1].wait()
        chosen(u_own, pu_ref)
        first_sends(1)
        loads[2].wait()
        chosen(a_own, a_mine)
        for other in range(row_devices):
            if other != owner:
                a_piece(other).start()
        a_got[...] = a_mine[owner * share:(owner + 1) * share, :]

    @pl.when(jnp.logical_not(is_owner))
    def _():
        loads[1].wait()
        loads[2].wait()

    def relay(kind, tick):
        for way in range(2):
            i = tick - SKEW * jnp.maximum(hops[way] - 1, 0)

            @pl.when(jnp.logical_and(jnp.logical_not(is_owner), jnp.logical_and(i >= 0, i < pieces)))
            def _():
                move(kind, way, core, i, nexts[way], 0).wait_recv()

                @pl.when(hops[way] < chips - 1)
                def _():
                    move(kind, way, core, i, nexts[way], 0).start()

                @pl.when(away)
                def _():
                    move(kind, way, core, i, pair, 1).start()

    def gather(kind):
        @pl.when(jnp.logical_not(is_owner))
        def _():
            @pl.loop(0, pieces)
            def _(i):
                for way in range(2):
                    move(kind, way, 1 - core, i, pair, 1).wait_recv()

    ticks = pieces + SKEW * max(chips - 2, 0)

    @pl.loop(0, ticks)
    def _(tick):
        relay(0, tick)

    gather(0)
    each = max(1, ticks // (blocks * slots))
    during = min(ticks, each * blocks * slots)

    @pl.loop(0, blocks)
    def _(b):
        at = window(b * rank, rank)
        pvt[at, :] = pv[:, at].T
        pin[:, at] = jnp.dot(pvt[at, :], pv[:, at], preferred_element_type=F32).astype(BF16)

        @pl.loop(0, slots)
        def _(t):
            here = window(t * tile, tile)
            inner = jnp.dot(pvt[at, :], v_own[here, at], preferred_element_type=F32).astype(BF16)
            left_ref[here, at] = lax.dot_general(
                u_own[here, at], inner, TRANS, preferred_element_type=F32
            ).astype(BF16)
            done = (b * slots + t) * each

            @pl.loop(jnp.minimum(done, during), jnp.minimum(done + each, during))
            def _(tick):
                relay(1, tick)

    @pl.loop(during, ticks)
    def _(tick):
        relay(1, tick)

    gather(1)

    rows = window(me * share, share)
    small = [
        lax.dot_general(
            pu_ref[rows, b * rank:(b + 1) * rank], pin[:, b * rank:(b + 1) * rank], TRANS,
            preferred_element_type=F32,
        ).astype(BF16)
        for b in range(blocks)
    ]
    small = jnp.concatenate(small, axis=1)
    part_ref[...] = -lax.dot_general(small, pu_ref[...], TRANS, preferred_element_type=F32)
    @pl.when(jnp.logical_not(is_owner))
    def _():
        a_piece(owner).wait_recv()

    mine_cols = window(col * a_got.shape[1], a_got.shape[1])
    part_ref[:, mine_cols] = part_ref[:, mine_cols] + a_got[...]

    @pl.when(is_owner)
    def _():
        for kind in range(2):

            @pl.loop(0, pieces)
            def _(i):
                for way in range(2):
                    move(kind, way, home_core, i, nexts[way], 0).wait_send()
                    move(kind, way, home_core, i, owner ^ 1, 1).wait_send()
                    move(kind, way, 1 - home_core, i, owner ^ 1, 2).wait_send()

        for other in range(row_devices):
            if other != owner:
                a_piece(other).wait_send()

    @pl.when(jnp.logical_not(is_owner))
    def _():
        for kind in range(2):

            @pl.loop(0, pieces)
            def _(i):
                for way in range(2):

                    @pl.when(hops[way] < chips - 1)
                    def _():
                        move(kind, way, core, i, nexts[way], 0).wait_send()

                    @pl.when(away)
                    def _():
                        move(kind, way, core, i, pair, 1).wait_send()


def spread(mesh, owner, mask, v, u, tiles):
    row_devices = mesh.shape["row"]
    tile, width = TILE, v.shape[1]
    pieces = 8
    share = tile // row_devices
    return pl.pallas_call(
        functools.partial(spread_kernel, owner, row_devices, pieces),
        out_shape=(
            jax.ShapeDtypeStruct(u.shape, BF16),
            jax.ShapeDtypeStruct((tile, width), BF16),
            jax.ShapeDtypeStruct((share, tile), F32),
        ),
        in_specs=[VM, ANY, ANY, ANY],
        out_specs=(VM, VM, VM),
        scratch_shapes=[
            pltpu.VMEM((tile, width), BF16),
            pltpu.VMEM(v.shape, BF16),
            pltpu.VMEM(u.shape, BF16),
            pltpu.VMEM(tiles.shape, F32),
            pltpu.VMEM((width, tile), BF16),
            pltpu.VMEM((RANK, width), BF16),
            pltpu.VMEM((tile, tiles.shape[1]), F32),
            pltpu.VMEM((share, tiles.shape[1]), F32),
            pltpu.SemaphoreType.DMA((2, 3, 2, pieces)),
            pltpu.SemaphoreType.DMA((2, 2, 2, pieces)),
            pltpu.SemaphoreType.DMA((row_devices,)),
            pltpu.SemaphoreType.DMA,
            pltpu.SemaphoreType.DMA((3,)),
        ],
        compiler_params=pltpu.CompilerParams(
            collective_id=1 + owner, has_side_effects=True, vmem_limit_bytes=48 * 1024 * 1024
        ),
        cost_estimate=pl.CostEstimate(flops=20_000_000_000, bytes_accessed=30_000_000, transcendentals=0),
        name="spread",
    )(mask, v, u, tiles)


def eliminate(block):
    shape = (SUB, BLK)
    groups = [block[g * SUB:(g + 1) * SUB, :] for g in range(BLK // SUB)]
    lane = lax.broadcasted_iota(jnp.int32, shape, 1)
    sub = lax.broadcasted_iota(jnp.int32, shape, 0)
    for g in range(len(groups)):
        base = g * SUB
        rows = groups[g]
        cols = [jnp.broadcast_to(rows[:, base + j:base + j + 1], shape) for j in range(SUB)]
        out = rows
        for s in range(SUB):
            raw = jnp.broadcast_to(rows[s:s + 1, :], shape)
            here = lane == base + s
            mine = sub == s
            out = jnp.where(mine, raw, out)
            inverse = 1.0 / jnp.broadcast_to(cols[s][s:s + 1, :], shape)
            factor = jnp.where(mine, 0.0, cols[s] * inverse)
            unit = jnp.where(here, 1.0, raw)
            kept = jnp.where(here, 0.0, rows)
            rows = jnp.where(mine, unit * inverse, kept - factor * unit)
            for j in range(s + 1, SUB):
                head = jnp.broadcast_to(cols[j][s:s + 1, :], shape)
                cols[j] = jnp.where(mine, head * inverse, cols[j] - factor * head)
        groups[g] = out
        if g + 1 == len(groups):
            break
        reduced = [jnp.broadcast_to(rows[s:s + 1, :], shape) for s in range(SUB)]
        inside = jnp.logical_and(lane >= base, lane < base + SUB)
        for h in range(g + 1, len(groups)):
            old = groups[h]
            terms = [
                jnp.broadcast_to(old[:, base + s:base + s + 1], shape) * reduced[s] for s in range(SUB)
            ]
            while len(terms) > 1:
                terms = [terms[i] + terms[i + 1] for i in range(0, len(terms), 2)]
            groups[h] = jnp.where(inside, 0.0, old) - terms[0]
    return jnp.concatenate(groups, axis=0)


def factor_step(k, w_ref, l_ref, x_ref):
    size = w_ref.shape[0]
    count = size // BLK
    row_id = lax.broadcasted_iota(jnp.int32, (BLK, BLK), 0)
    col_id = lax.broadcasted_iota(jnp.int32, (BLK, BLK), 1)
    at = window(k * BLK, BLK)
    done = eliminate(w_ref[at, at])
    pivots = jnp.sum(jnp.where(row_id == col_id, done, 0.0), axis=1, keepdims=True)
    scale = 1.0 / jnp.sqrt(pivots)
    upper = jnp.where(col_id >= row_id, done * scale, 0.0)
    inner = jnp.where(col_id < row_id, done * scale, 0.0) + jnp.where(row_id == col_id, scale, 0.0)
    l_ref[at, at] = upper.T
    row = dot(inner, w_ref[at, :])
    block_id = lax.broadcasted_iota(jnp.int32, (BLK, size), 1) // BLK
    row = jnp.where(block_id == k, jnp.concatenate([inner] * count, axis=1), row)
    x_ref[at, :] = jnp.where(block_id <= k, row, 0.0)
    inner_t = inner.T

    strip_row = lax.broadcasted_iota(jnp.int32, (STRIP, BLK), 0) // BLK
    per = STRIP // BLK

    @pl.loop((k + 1) // per, count // per)
    def _(i):
        there = window(i * STRIP, STRIP)
        below = strip_row + i * per > k
        old = w_ref[there, at]
        left = jnp.where(below, dot(old, inner_t), 0.0)
        l_ref[there, at] = jnp.where(below, left, l_ref[there, at])
        w_ref[there, at] = jnp.where(below, 0.0, old)
        w_ref[there, :] = w_ref[there, :] - dot(left, row)


def panel_kernel(
    depth, row_devices, pieces, chunks, part_ref, left_ref, u_ref, a_ref, out_ref, lcol_ref,
    w_ref, l_ref, x_ref, acc, come, got,
    sends, recvs, pair_send, pair_recv, line_send, line_recv, out_send, out_recv,
):
    me = lax.axis_index("row")
    col = lax.axis_index("col")
    chips = row_devices // 2
    chip, core = me // 2, me % 2
    share = part_ref.shape[0]
    sub = share // depth
    pair = chip * 2 + 1 - core
    cols = [(col + d) % depth for d in range(1, depth)]
    peers = [((chip + d) % chips) * 2 + core for d in range(1, chips)]
    size = w_ref.shape[0]
    width = a_ref.shape[1]
    half = acc.shape[0] // 2
    piece = half // pieces
    count = size // BLK

    barrier = pltpu.get_barrier_semaphore()
    for other in cols:
        pl.semaphore_signal(barrier, inc=1, device_id=(me, other), device_id_type=MESH)
    for other in peers + [pair]:
        pl.semaphore_signal(barrier, inc=1, device_id=(other, col), device_id_type=MESH)
    pl.semaphore_wait(barrier, depth + chips - 1)

    def groups_of(holder):
        return ((holder + 1) * share - 1) // GROUP + 1

    def over(holder, act):
        @pl.loop(0, groups_of(holder))
        def _(g):
            act(g, window(g * GROUP, GROUP))

    mine = window(me * share + col * sub, sub)

    def first(d, g, at):
        return remote(
            part_ref.at[window(cols[d] * sub, sub), at], got.at[d, :, at], sends.at[d, g], recvs.at[d, g], (me, cols[d])
        )

    def second(d, g, at):
        n = depth - 1 + d
        ref = w_ref.at[mine, at]
        return remote(ref, ref, sends.at[n, g], recvs.at[n, g], (me, cols[d]))

    def third(d, holder, g, at):
        n = 2 * (depth - 1) + d
        ref = w_ref.at[window(holder * share, share), at]
        return remote(ref, ref, sends.at[n, g], recvs.at[n, g], (peers[d], col))

    def fourth(d, holder, g, at):
        ref = w_ref.at[window(holder * share, share), at]
        return remote(ref, ref, pair_send.at[d, g], pair_recv.at[d, g], (pair, col))

    holders = [((chip + chips - d) % chips) * 2 + core for d in range(chips)]
    others = [((chip + chips - d) % chips) * 2 + 1 - core for d in range(chips)]
    for d in range(depth - 1):
        over(me, lambda g, at: first(d, g, at).start())

    mine_cols = window(col * width, width)
    strips = half // FILL

    def fill(q):
        for way in range(2):
            at = slice(way * half + q * FILL, way * half + (q + 1) * FILL)
            acc[at, :] = -lax.dot_general(left_ref[at, :], u_ref[...], TRANS, preferred_element_type=F32)
            acc[at, mine_cols] = acc[at, mine_cols] + a_ref[at, :]

    def line(way, i, target):
        at = window(way * half + i * piece, piece)
        return remote(acc.at[at, :], come.at[at, :], line_send.at[way, i], line_recv.at[way, i], (me, target))

    def pass_on(way, i, seat, target):
        @pl.when(jnp.logical_and(i >= 0, i < pieces))
        def _():
            at = window(way * half + i * piece, piece)

            @pl.when(seat > 0)
            def _():
                line(way, i, target).wait_recv()
                acc[at, :] = acc[at, :] + come[at, :]

            @pl.when(seat < depth - 1)
            def _():
                line(way, i, target).start()

    up = jnp.minimum(col + 1, depth - 1)
    down = jnp.maximum(col - 1, 0)
    seat_down = depth - 1 - col

    def line_step(tick):
        pass_on(0, tick - seat_down, seat_down, down)
        pass_on(1, tick - col, col, up)

    def line_steps(lo, hi):
        @pl.loop(lo, hi)
        def _(tick):
            line_step(tick)

    def sum_share():
        def act(g, at):
            total = part_ref[window(col * sub, sub), at]
            for d in range(depth - 1):
                first(d, g, at).wait_recv()
                total = total + got[d, :, at]
            w_ref[mine, at] = total
            for d in range(depth - 1):
                second(d, g, at).start()

        over(me, act)

    def to_peers():
        def act(g, at):
            for d in range(depth - 1):
                second(d, g, at).wait_recv()
            for d in range(chips - 1):
                third(d, me, g, at).start()
            fourth(0, me, g, at).start()

        over(me, act)

    def to_pair(d):
        def act(g, at):
            third(d - 1, holders[d], g, at).wait_recv()
            fourth(d, holders[d], g, at).start()

        over(holders[d], act)

    ticks = pieces + depth - 1
    per = pieces // strips
    state = {"tick": 0, "fill": 0}

    def advance(n):
        for _ in range(n):
            if state["tick"] >= ticks:
                return
            while state["fill"] < strips and state["fill"] * per <= state["tick"] + 1:
                fill(state["fill"])
                state["fill"] += 1
            line_steps(state["tick"], state["tick"] + 1)
            state["tick"] += 1

    advance(2)
    sum_share()
    advance(2)
    to_peers()
    advance(2)
    for d in range(1, chips):
        to_pair(d)
        if d < 4:
            advance(1)
    while state["fill"] < strips:
        fill(state["fill"])
        state["fill"] += 1
    for d in range(chips):
        over(others[d], lambda g, at: fourth(d, others[d], g, at).wait_recv())
    for d in range(depth - 1):
        over(me, lambda g, at: first(d, g, at).wait_send())
        over(me, lambda g, at: second(d, g, at).wait_send())
    for d in range(chips - 1):
        over(me, lambda g, at: third(d, me, g, at).wait_send())
    for d in range(chips):
        over(holders[d], lambda g, at: fourth(d, holders[d], g, at).wait_send())

    @pl.loop(0, count)
    def _(i):
        at = window(i * BLK, BLK)
        l_ref[at, :] = jnp.zeros((BLK, size), F32)
        w_ref[at, at] = (w_ref[at, at] + w_ref[at, at].T) * 0.5

        @pl.loop(i + 1, count)
        def _(j):
            there = window(j * BLK, BLK)
            w_ref[at, there] = w_ref[there, at].T

    ready = state["tick"]
    left_ticks = ticks - ready

    @pl.loop(0, count)
    def _(k):
        line_steps(ready + k * left_ticks // count, ready + (k + 1) * left_ticks // count)
        factor_step(k, w_ref, l_ref, x_ref)

    lcol_ref[...] = l_ref[:, mine_cols]

    chunk = half // chunks

    def deal(way, i, c):
        at = window(way * half + i * chunk, chunk)
        return remote(
            come.at[at, c * width:(c + 1) * width], out_ref.at[at, :],
            out_send.at[i, c], out_recv.at[way, i], (me, c),
        )

    ends = [(0, 0), (1, depth - 1)]
    for way, end in ends:

        @pl.when(col == end)
        def _():
            @pl.loop(0, chunks)
            def _(i):
                at = window(way * half + i * chunk, chunk)
                for c in sorted(range(depth), key=lambda c: -abs(c - end)):
                    upto = (c + 1) * width
                    value = dot(acc[at, :upto], x_ref[c * width:upto, :upto], ((1,), (1,)))
                    if c == end:
                        out_ref[at, :] = value
                    else:
                        come[at, c * width:upto] = value
                        deal(way, i, c).start()

    for way, end in ends:

        @pl.when(col != end)
        def _():
            @pl.loop(0, chunks)
            def _(i):
                deal(way, i, 0).wait_recv()

    for way, end in ends:

        @pl.when(col == end)
        def _():
            @pl.loop(0, chunks)
            def _(i):
                for c in range(depth):
                    if c != end:
                        deal(way, i, c).wait_send()

    @pl.when(col > 0)
    def _():
        @pl.loop(0, pieces)
        def _(i):
            line(0, i, down).wait_send()

    @pl.when(col < depth - 1)
    def _():
        @pl.loop(0, pieces)
        def _(i):
            line(1, i, up).wait_send()


def panel(mesh, part, left, pivot_u, tiles):
    row_devices, depth = mesh.shape["row"], mesh.shape["col"]
    chips = row_devices // 2
    share, size = part.shape
    rows, width = tiles.shape
    pieces = rows // 2 // 64
    chunks = rows // 2 // 128
    links = 2 * (depth - 1) + chips - 1
    return pl.pallas_call(
        functools.partial(panel_kernel, depth, row_devices, pieces, chunks),
        out_shape=(
            jax.ShapeDtypeStruct((rows, width), F32),
            jax.ShapeDtypeStruct((size, width), F32),
        ),
        in_specs=[VM] * 4,
        out_specs=(VM, VM),
        scratch_shapes=[
            pltpu.VMEM((size, size), F32),
            pltpu.VMEM((size, size), F32),
            pltpu.VMEM((size, size), F32),
            pltpu.VMEM((rows, size), F32),
            pltpu.VMEM((rows, size), F32),
            pltpu.VMEM((depth - 1, share // depth, size), F32),
            pltpu.SemaphoreType.DMA((links, size // GROUP)),
            pltpu.SemaphoreType.DMA((links, size // GROUP)),
            pltpu.SemaphoreType.DMA((chips, size // GROUP)),
            pltpu.SemaphoreType.DMA((chips, size // GROUP)),
            pltpu.SemaphoreType.DMA((2, pieces)),
            pltpu.SemaphoreType.DMA((2, pieces)),
            pltpu.SemaphoreType.DMA((chunks, depth)),
            pltpu.SemaphoreType.DMA((2, chunks)),
        ],
        compiler_params=pltpu.CompilerParams(
            collective_id=0, has_side_effects=True, vmem_limit_bytes=58 * 1024 * 1024
        ),
        cost_estimate=pl.CostEstimate(flops=60_000_000_000, bytes_accessed=30_000_000, transcendentals=0),
        name="panel",
    )(part, left, pivot_u, tiles)


def local(mesh, panel_tiles, left_u, earlier_right_factors, tile_global_index):
    row_devices = mesh.shape["row"]
    tile_count = tile_global_index.shape[0]
    slots = panel_tiles.shape[0] // TILE
    pivot_position = jnp.sum(
        jnp.where(tile_global_index == 0, jnp.arange(tile_count, dtype=jnp.int32), 0)
    )
    owner_row = pivot_position // slots
    local_slot = pivot_position % slots

    mask = jnp.arange(slots, dtype=jnp.int32)[:, None] == local_slot
    mask = jnp.broadcast_to(mask.astype(F32), (slots, left_u.shape[1]))
    branches = [functools.partial(spread, mesh, owner) for owner in range(row_devices)]
    left, pivot_u, part = lax.switch(
        owner_row, branches, mask, earlier_right_factors, left_u, panel_tiles,
    )
    solved, chol = panel(mesh, part, left, pivot_u, panel_tiles)
    chosen = jnp.logical_and(lax.axis_index("row") == owner_row, jnp.arange(slots) == local_slot)
    solved = solved.reshape(slots, TILE, -1)
    return jnp.where(chosen[:, None, None], chol[None], solved).reshape(panel_tiles.shape)


def solution(mesh):
    in_specs = (P("row", "col"), P("row", "col"), P("row", "col"), P())
    return jax.shard_map(
        functools.partial(local, mesh), mesh=mesh, in_specs=in_specs, out_specs=P("row", "col"), check_vma=False
    )
```

```python
import functools

import jax
import jax.numpy as jnp
from jax import lax
from jax.experimental import pallas as pl
from jax.experimental.pallas import tpu as pltpu
from jax.sharding import PartitionSpec as P

TILE = 1024
RANK = 256

BLK = 128
SUB = 8
FILL = 256
STRIP = 256
GROUP = 256
SKEW = 3
LAG = 2
F32 = jnp.float32
BF16 = jnp.bfloat16
HI = lax.Precision.HIGHEST
MESH = pl.DeviceIdType.MESH
ANY = pl.BlockSpec(memory_space=pl.ANY)
VM = pl.BlockSpec(memory_space=pltpu.VMEM)
TRANS = (((1,), (1,)), ((), ()))


def dot(a, b, dims=((1,), (0,))):
    return lax.dot_general(a, b, (dims, ((), ())), precision=HI, preferred_element_type=F32)


def window(start, size):
    return pl.ds(pl.multiple_of(start, size), size)


def remote(src, dst, send, recv, target):
    return pltpu.make_async_remote_copy(
        src_ref=src, dst_ref=dst, send_sem=send, recv_sem=recv, device_id=target, device_id_type=MESH
    )


def pick(table, index):
    value = jnp.int32(table[0])
    for i in range(1, len(table)):
        value = jnp.where(index == i, jnp.int32(table[i]), value)
    return value


def spread_kernel(
    owner, row_devices, pieces, mask_ref, v_ref, u_ref, a_ref, left_ref, pu_ref, part_ref,
    pv, v_own, u_own, a_own, pvt, pin, left_own, small, a_mine, a_got, sends, recvs, a_send, a_recv, local_sem,
):
    me = lax.axis_index("row")
    col = lax.axis_index("col")
    chips = row_devices // 2
    chip, core = me // 2, me % 2
    order = [i ^ (i >> 1) for i in range(chips)]
    if max(order) >= chips:
        order = list(range(chips))
    home = order.index(owner // 2)
    home_core = owner % 2
    place = pick([order.index(c) for c in range(chips)], chip)
    nexts = [pick(order, (place + chips + w) % chips) * 2 + core for w in (1, -1)]
    hops = [(chips + w * (place - home)) % chips for w in (1, -1)]
    pair = chip * 2 + 1 - core
    tile, width = pu_ref.shape
    half = tile // 2
    step = half // (2 * pieces)
    share = tile // row_devices
    rank = RANK
    blocks = width // rank
    slots = v_ref.shape[0] // tile

    loads = [
        pltpu.make_async_copy(src, dst, local_sem.at[i])
        for i, (src, dst) in enumerate(((v_ref, v_own), (u_ref, u_own), (a_ref, a_own)))
    ]
    loads[0].start()

    barrier = pltpu.get_barrier_semaphore()
    for d in range(1, row_devices):
        pl.semaphore_signal(barrier, inc=1, device_id=((me + d) % row_devices, col), device_id_type=MESH)
    pl.semaphore_wait(barrier, row_devices - 1)
    loads[0].wait()
    loads[1].start()
    loads[2].start()

    bufs = (pv, pu_ref)

    def move(kind, way, side, i, target, lane):
        at = window(way * half + (2 * i + side) * step, step)
        ref = bufs[kind].at[at, :]
        return remote(ref, ref, sends.at[kind, lane, way, i], recvs.at[kind, way, side, i], (target, col))

    is_owner = me == owner
    away = chip != owner // 2
    helper = jnp.logical_and(jnp.logical_not(away), jnp.logical_not(is_owner))

    def a_piece(target):
        return remote(a_mine.at[window(target * share, share), :], a_got, a_send.at[target], a_recv, (target, col))

    def chosen(src, dst):
        @pl.loop(0, tile // BLK)
        def _(n):
            total = None
            for t in range(slots):
                keep = mask_ref[t:t + 1, :dst.shape[1]].astype(dst.dtype)
                term = src[window(t * tile + n * BLK, BLK), :] * keep
                total = term if total is None else total + term
            dst[window(n * BLK, BLK), :] = total

    def first_sends(kind):
        @pl.loop(0, pieces)
        def _(i):
            for way in range(2):
                move(kind, way, 1 - home_core, i, owner ^ 1, 2).start()
                move(kind, way, home_core, i, nexts[way], 0).start()
            for way in range(2):
                move(kind, way, home_core, i, owner ^ 1, 1).start()

    @pl.when(is_owner)
    def _():
        chosen(v_own, pv)
        first_sends(0)
        loads[1].wait()
        chosen(u_own, pu_ref)
        first_sends(1)
        loads[2].wait()
        chosen(a_own, a_mine)
        for other in range(row_devices):
            if other != owner:
                a_piece(other).start()
        a_got[...] = a_mine[owner * share:(owner + 1) * share, :]

    @pl.when(jnp.logical_not(is_owner))
    def _():
        loads[1].wait()
        loads[2].wait()

    def relay(kind, tick):
        for way in range(2):
            i = tick - SKEW * jnp.maximum(hops[way] - 1, 0)

            @pl.when(jnp.logical_and(jnp.logical_not(is_owner), jnp.logical_and(i >= 0, i < pieces)))
            def _():
                move(kind, way, core, i, nexts[way], 0).wait_recv()

                @pl.when(hops[way] < chips - 1)
                def _():
                    move(kind, way, core, i, nexts[way], 0).start()

                @pl.when(away)
                def _():
                    move(kind, way, core, i, pair, 1).start()

    def gather(kind):
        @pl.when(jnp.logical_not(is_owner))
        def _():
            @pl.loop(0, pieces)
            def _(i):
                for way in range(2):
                    move(kind, way, 1 - core, i, pair, 1).wait_recv()

    ticks = pieces + SKEW * max(chips - 2, 0)

    @pl.loop(0, ticks)
    def _(tick):
        relay(0, tick)

    gather(0)
    each = max(1, ticks // (blocks * slots))
    during = min(ticks, each * blocks * slots)

    @pl.loop(0, blocks)
    def _(b):
        at = window(b * rank, rank)
        pvt[at, :] = pv[:, at].T
        pin[:, at] = jnp.dot(pvt[at, :], pv[:, at], preferred_element_type=F32).astype(BF16)

        @pl.loop(0, slots)
        def _(t):
            here = window(t * tile, tile)
            inner = jnp.dot(pvt[at, :], v_own[here, at], preferred_element_type=F32).astype(BF16)
            left_own[here, at] = lax.dot_general(
                u_own[here, at], inner, TRANS, preferred_element_type=F32
            ).astype(BF16)
            done = (b * slots + t) * each

            @pl.loop(jnp.minimum(done, during), jnp.minimum(done + each, during))
            def _(tick):
                relay(1, tick)

    left_out = pltpu.make_async_copy(left_own, left_ref, local_sem.at[3])
    left_out.start()

    @pl.loop(during, ticks)
    def _(tick):
        relay(1, tick)

    gather(1)
    rows = window(me * share, share)

    @pl.loop(0, blocks)
    def _(b):
        at = window(b * rank, rank)
        small[:, at] = lax.dot_general(
            pu_ref[rows, at], pin[:, at], TRANS, preferred_element_type=F32
        ).astype(BF16)

    @pl.loop(0, tile // rank)
    def _(n):
        at = window(n * rank, rank)
        part_ref[:, at] = -lax.dot_general(small[...], pu_ref[at, :], TRANS, preferred_element_type=F32)

    @pl.when(jnp.logical_not(is_owner))
    def _():
        a_piece(owner).wait_recv()

    mine_cols = window(col * a_got.shape[1], a_got.shape[1])
    part_ref[:, mine_cols] = part_ref[:, mine_cols] + a_got[...]
    left_out.wait()

    @pl.when(is_owner)
    def _():
        for kind in range(2):

            @pl.loop(0, pieces)
            def _(i):
                for way in range(2):
                    move(kind, way, home_core, i, nexts[way], 0).wait_send()
                    move(kind, way, home_core, i, owner ^ 1, 1).wait_send()
                    move(kind, way, 1 - home_core, i, owner ^ 1, 2).wait_send()

        for other in range(row_devices):
            if other != owner:
                a_piece(other).wait_send()

    @pl.when(jnp.logical_not(is_owner))
    def _():
        for kind in range(2):

            @pl.loop(0, pieces)
            def _(i):
                for way in range(2):

                    @pl.when(hops[way] < chips - 1)
                    def _():
                        move(kind, way, core, i, nexts[way], 0).wait_send()

                    @pl.when(away)
                    def _():
                        move(kind, way, core, i, pair, 1).wait_send()


def spread(mesh, owner, mask, v, u, tiles):
    row_devices = mesh.shape["row"]
    tile, width = TILE, v.shape[1]
    pieces = 8
    share = tile // row_devices
    return pl.pallas_call(
        functools.partial(spread_kernel, owner, row_devices, pieces),
        out_shape=(
            jax.ShapeDtypeStruct(u.shape, BF16),
            jax.ShapeDtypeStruct((tile, width), BF16),
            jax.ShapeDtypeStruct((share, tile), F32),
        ),
        in_specs=[VM, ANY, ANY, ANY],
        out_specs=(ANY, VM, VM),
        scratch_shapes=[
            pltpu.VMEM((tile, width), BF16),
            pltpu.VMEM(v.shape, BF16),
            pltpu.VMEM(u.shape, BF16),
            pltpu.VMEM(tiles.shape, F32),
            pltpu.VMEM((width, tile), BF16),
            pltpu.VMEM((RANK, width), BF16),
            pltpu.VMEM(u.shape, BF16),
            pltpu.VMEM((share, width), BF16),
            pltpu.VMEM((tile, tiles.shape[1]), F32),
            pltpu.VMEM((share, tiles.shape[1]), F32),
            pltpu.SemaphoreType.DMA((2, 3, 2, pieces)),
            pltpu.SemaphoreType.DMA((2, 2, 2, pieces)),
            pltpu.SemaphoreType.DMA((row_devices,)),
            pltpu.SemaphoreType.DMA,
            pltpu.SemaphoreType.DMA((4,)),
        ],
        compiler_params=pltpu.CompilerParams(
            collective_id=1 + owner, has_side_effects=True, vmem_limit_bytes=48 * 1024 * 1024
        ),
        cost_estimate=pl.CostEstimate(flops=20_000_000_000, bytes_accessed=30_000_000, transcendentals=0),
        name="spread",
    )(mask, v, u, tiles)


def eliminate(block):
    shape = (SUB, BLK)
    groups = [block[g * SUB:(g + 1) * SUB, :] for g in range(BLK // SUB)]
    lane = lax.broadcasted_iota(jnp.int32, shape, 1)
    sub = lax.broadcasted_iota(jnp.int32, shape, 0)
    for g in range(len(groups)):
        base = g * SUB
        rows = groups[g]
        cols = [jnp.broadcast_to(rows[:, base + j:base + j + 1], shape) for j in range(SUB)]
        out = rows
        for s in range(SUB):
            raw = jnp.broadcast_to(rows[s:s + 1, :], shape)
            here = lane == base + s
            mine = sub == s
            out = jnp.where(mine, raw, out)
            inverse = 1.0 / jnp.broadcast_to(cols[s][s:s + 1, :], shape)
            factor = jnp.where(mine, 0.0, cols[s] * inverse)
            unit = jnp.where(here, 1.0, raw)
            kept = jnp.where(here, 0.0, rows)
            rows = jnp.where(mine, unit * inverse, kept - factor * unit)
            for j in range(s + 1, SUB):
                head = jnp.broadcast_to(cols[j][s:s + 1, :], shape)
                cols[j] = jnp.where(mine, head * inverse, cols[j] - factor * head)
        groups[g] = out
        if g + 1 == len(groups):
            break
        reduced = [jnp.broadcast_to(rows[s:s + 1, :], shape) for s in range(SUB)]
        inside = jnp.logical_and(lane >= base, lane < base + SUB)
        for h in range(g + 1, len(groups)):
            old = groups[h]
            terms = [
                jnp.broadcast_to(old[:, base + s:base + s + 1], shape) * reduced[s] for s in range(SUB)
            ]
            while len(terms) > 1:
                terms = [terms[i] + terms[i + 1] for i in range(0, len(terms), 2)]
            groups[h] = jnp.where(inside, 0.0, old) - terms[0]
    return jnp.concatenate(groups, axis=0)


def factor_step(k, w_ref, l_ref, x_ref):
    size = w_ref.shape[0]
    count = size // BLK
    row_id = lax.broadcasted_iota(jnp.int32, (BLK, BLK), 0)
    col_id = lax.broadcasted_iota(jnp.int32, (BLK, BLK), 1)
    at = window(k * BLK, BLK)
    done = eliminate(w_ref[at, at])
    pivots = jnp.sum(jnp.where(row_id == col_id, done, 0.0), axis=1, keepdims=True)
    scale = 1.0 / jnp.sqrt(pivots)
    upper = jnp.where(col_id >= row_id, done * scale, 0.0)
    inner = jnp.where(col_id < row_id, done * scale, 0.0) + jnp.where(row_id == col_id, scale, 0.0)
    l_ref[at, at] = upper.T
    row = dot(inner, w_ref[at, :])
    block_id = lax.broadcasted_iota(jnp.int32, (BLK, size), 1) // BLK
    row = jnp.where(block_id == k, jnp.concatenate([inner] * count, axis=1), row)
    x_ref[at, :] = jnp.where(block_id <= k, row, 0.0)
    inner_t = inner.T

    strip_row = lax.broadcasted_iota(jnp.int32, (STRIP, BLK), 0) // BLK
    per = STRIP // BLK

    @pl.loop((k + 1) // per, count // per)
    def _(i):
        there = window(i * STRIP, STRIP)
        below = strip_row + i * per > k
        old = w_ref[there, at]
        left = jnp.where(below, dot(old, inner_t), 0.0)
        l_ref[there, at] = jnp.where(below, left, l_ref[there, at])
        w_ref[there, at] = jnp.where(below, 0.0, old)
        w_ref[there, :] = w_ref[there, :] - dot(left, row)


def panel_kernel(
    depth, row_devices, pieces, chunks, part_ref, left_ref, u_ref, a_ref, out_ref, lcol_ref,
    w_ref, l_ref, x_ref, acc, come, got, left_own, local_sem,
    sends, recvs, pair_send, pair_recv, line_send, line_recv, out_send, out_recv,
):
    me = lax.axis_index("row")
    col = lax.axis_index("col")
    chips = row_devices // 2
    chip, core = me // 2, me % 2
    share = part_ref.shape[0]
    sub = share // depth
    pair = chip * 2 + 1 - core
    cols = [(col + d) % depth for d in range(1, depth)]
    peers = [((chip + d) % chips) * 2 + core for d in range(1, chips)]
    size = w_ref.shape[0]
    width = a_ref.shape[1]
    half = acc.shape[0] // 2
    piece = half // pieces
    count = size // BLK
    load = pltpu.make_async_copy(left_ref, left_own, local_sem)
    load.start()

    barrier = pltpu.get_barrier_semaphore()
    for other in cols:
        pl.semaphore_signal(barrier, inc=1, device_id=(me, other), device_id_type=MESH)
    for other in peers + [pair]:
        pl.semaphore_signal(barrier, inc=1, device_id=(other, col), device_id_type=MESH)
    pl.semaphore_wait(barrier, depth + chips - 1)

    def groups_of(holder):
        return ((holder + 1) * share - 1) // GROUP + 1

    def over(holder, act):
        @pl.loop(0, groups_of(holder))
        def _(g):
            act(g, window(g * GROUP, GROUP))

    mine = window(me * share + col * sub, sub)

    def first(d, g, at):
        return remote(
            part_ref.at[window(cols[d] * sub, sub), at], got.at[d, :, at], sends.at[d, g], recvs.at[d, g], (me, cols[d])
        )

    def second(d, g, at):
        n = depth - 1 + d
        ref = w_ref.at[mine, at]
        return remote(ref, ref, sends.at[n, g], recvs.at[n, g], (me, cols[d]))

    def third(d, holder, g, at):
        n = 2 * (depth - 1) + d
        ref = w_ref.at[window(holder * share, share), at]
        return remote(ref, ref, sends.at[n, g], recvs.at[n, g], (peers[d], col))

    def fourth(d, holder, g, at):
        ref = w_ref.at[window(holder * share, share), at]
        return remote(ref, ref, pair_send.at[d, g], pair_recv.at[d, g], (pair, col))

    holders = [((chip + chips - d) % chips) * 2 + core for d in range(chips)]
    others = [((chip + chips - d) % chips) * 2 + 1 - core for d in range(chips)]
    for d in range(depth - 1):
        over(me, lambda g, at: first(d, g, at).start())

    mine_cols = window(col * width, width)
    strips = half // FILL

    def fill(q):
        @pl.loop(0, 2)
        def _(way):
            at = window(way * half + q * FILL, FILL)
            acc[at, :] = -lax.dot_general(left_own[at, :], u_ref[...], TRANS, preferred_element_type=F32)
            acc[at, mine_cols] = acc[at, mine_cols] + a_ref[at, :]

    def line(way, i, target):
        at = window(way * half + i * piece, piece)
        return remote(acc.at[at, :], come.at[at, :], line_send.at[way, i], line_recv.at[way, i], (me, target))

    def pass_on(way, i, seat, target):
        @pl.when(jnp.logical_and(i >= 0, i < pieces))
        def _():
            at = window(way * half + i * piece, piece)

            @pl.when(seat > 0)
            def _():
                line(way, i, target).wait_recv()
                acc[at, :] = acc[at, :] + come[at, :]

            @pl.when(seat < depth - 1)
            def _():
                line(way, i, target).start()

    up = jnp.minimum(col + 1, depth - 1)
    down = jnp.maximum(col - 1, 0)
    seat_down = depth - 1 - col

    def line_step(tick):
        pass_on(0, tick - LAG * seat_down, seat_down, down)
        pass_on(1, tick - LAG * col, col, up)

    def line_steps(lo, hi):
        @pl.loop(lo, hi)
        def _(tick):
            line_step(tick)

    def sum_share():
        def act(g, at):
            total = part_ref[window(col * sub, sub), at]
            for d in range(depth - 1):
                first(d, g, at).wait_recv()
                total = total + got[d, :, at]
            w_ref[mine, at] = total
            for d in range(depth - 1):
                second(d, g, at).start()

        over(me, act)

    def to_peers():
        def act(g, at):
            for d in range(depth - 1):
                second(d, g, at).wait_recv()
            for d in range(chips - 1):
                third(d, me, g, at).start()
            fourth(0, me, g, at).start()

        over(me, act)

    def to_pair(d):
        def act(g, at):
            third(d - 1, holders[d], g, at).wait_recv()
            fourth(d, holders[d], g, at).start()

        over(holders[d], act)

    ticks = pieces + LAG * (depth - 1)
    load.wait()
    ready = max(6, strips)

    @pl.loop(0, ready)
    def _(tick):
        @pl.when(tick < strips)
        def _():
            fill(tick)

        @pl.when(tick == 0)
        def _():
            sum_share()

        line_step(tick)

        @pl.when(tick == 2)
        def _():
            to_peers()

        @pl.when(tick == 4)
        def _():
            for d in range(1, chips - 1):
                to_pair(d)

    to_pair(chips - 1)
    for d in range(chips):
        over(others[d], lambda g, at: fourth(d, others[d], g, at).wait_recv())
    for d in range(depth - 1):
        over(me, lambda g, at: first(d, g, at).wait_send())
        over(me, lambda g, at: second(d, g, at).wait_send())
    for d in range(chips - 1):
        over(me, lambda g, at: third(d, me, g, at).wait_send())
    for d in range(chips):
        over(holders[d], lambda g, at: fourth(d, holders[d], g, at).wait_send())

    @pl.loop(0, count)
    def _(i):
        at = window(i * BLK, BLK)
        l_ref[at, :] = jnp.zeros((BLK, size), F32)
        w_ref[at, at] = (w_ref[at, at] + w_ref[at, at].T) * 0.5

        @pl.loop(i + 1, count)
        def _(j):
            there = window(j * BLK, BLK)
            w_ref[at, there] = w_ref[there, at].T

    after = min(ticks, ready + count)

    @pl.loop(0, count)
    def _(k):
        line_steps(jnp.minimum(ready + k, after), jnp.minimum(ready + k + 1, after))
        factor_step(k, w_ref, l_ref, x_ref)

    chunk = half // chunks

    def deal(way, i, c):
        at = window(way * half + i * chunk, chunk)
        return remote(
            come.at[at, c * width:(c + 1) * width], out_ref.at[at, :],
            out_send.at[i, c], out_recv.at[way, i], (me, c),
        )

    ends = [(0, 0), (1, depth - 1)]
    at_end = jnp.logical_or(col == 0, col == depth - 1)
    own_way = jnp.where(col == 0, 0, 1)

    def reach(i):
        even = after + i * (ticks - after) // chunks
        need = i * (pieces // chunks) + LAG * (depth - 1)
        return jnp.minimum(ticks, jnp.maximum(even, jnp.where(i > 0, need, after)))

    @pl.loop(0, chunks)
    def _(i):
        line_steps(reach(i), reach(i + 1))

        @pl.when(at_end)
        def _():
            at = window(own_way * half + i * chunk, chunk)
            for c in reversed(range(depth)):
                upto = (c + 1) * width
                value = dot(acc[at, :upto], x_ref[c * width:upto, :upto], ((1,), (1,)))

                @pl.when(col == c)
                def _():
                    out_ref[at, :] = value

                @pl.when(col != c)
                def _():
                    come[at, c * width:upto] = value
                    deal(own_way, i, c).start()

    lcol_ref[...] = l_ref[:, mine_cols]

    for way, end in ends:

        @pl.when(col != end)
        def _():
            @pl.loop(0, chunks)
            def _(i):
                deal(way, i, 0).wait_recv()

    @pl.when(at_end)
    def _():
        @pl.loop(0, chunks)
        def _(i):
            for c in range(depth):

                @pl.when(col != c)
                def _():
                    deal(own_way, i, c).wait_send()

    @pl.when(col > 0)
    def _():
        @pl.loop(0, pieces)
        def _(i):
            line(0, i, down).wait_send()

    @pl.when(col < depth - 1)
    def _():
        @pl.loop(0, pieces)
        def _(i):
            line(1, i, up).wait_send()


def panel(mesh, part, left, pivot_u, tiles):
    row_devices, depth = mesh.shape["row"], mesh.shape["col"]
    chips = row_devices // 2
    share, size = part.shape
    rows, width = tiles.shape
    pieces = rows // 2 // 64
    chunks = rows // 2 // 128
    links = 2 * (depth - 1) + chips - 1
    return pl.pallas_call(
        functools.partial(panel_kernel, depth, row_devices, pieces, chunks),
        out_shape=(
            jax.ShapeDtypeStruct((rows, width), F32),
            jax.ShapeDtypeStruct((size, width), F32),
        ),
        in_specs=[VM, ANY, VM, VM],
        out_specs=(VM, VM),
        scratch_shapes=[
            pltpu.VMEM((size, size), F32),
            pltpu.VMEM((size, size), F32),
            pltpu.VMEM((size, size), F32),
            pltpu.VMEM((rows, size), F32),
            pltpu.VMEM((rows, size), F32),
            pltpu.VMEM((depth - 1, share // depth, size), F32),
            pltpu.VMEM(left.shape, BF16),
            pltpu.SemaphoreType.DMA,
            pltpu.SemaphoreType.DMA((links, size // GROUP)),
            pltpu.SemaphoreType.DMA((links, size // GROUP)),
            pltpu.SemaphoreType.DMA((chips, size // GROUP)),
            pltpu.SemaphoreType.DMA((chips, size // GROUP)),
            pltpu.SemaphoreType.DMA((2, pieces)),
            pltpu.SemaphoreType.DMA((2, pieces)),
            pltpu.SemaphoreType.DMA((chunks, depth)),
            pltpu.SemaphoreType.DMA((2, chunks)),
        ],
        compiler_params=pltpu.CompilerParams(
            collective_id=0, has_side_effects=True, vmem_limit_bytes=58 * 1024 * 1024
        ),
        cost_estimate=pl.CostEstimate(flops=60_000_000_000, bytes_accessed=30_000_000, transcendentals=0),
        name="panel",
    )(part, left, pivot_u, tiles)


def local(mesh, panel_tiles, left_u, earlier_right_factors, tile_global_index):
    row_devices = mesh.shape["row"]
    tile_count = tile_global_index.shape[0]
    slots = panel_tiles.shape[0] // TILE
    here = tile_global_index == 0
    position = jnp.arange(tile_count, dtype=jnp.int32)
    owner_row = jnp.sum(jnp.where(here, position // slots, 0))
    mask = jnp.logical_and(here[None, :], (position % slots)[None, :] == jnp.arange(slots)[:, None])
    mask = jnp.sum(mask.astype(F32), axis=1)
    local_slot = jnp.sum(jnp.where(here, position % slots, 0))
    mask = jnp.broadcast_to(mask[:, None], (slots, left_u.shape[1]))
    branches = [functools.partial(spread, mesh, owner) for owner in range(row_devices)]
    left, pivot_u, part = lax.switch(
        owner_row, branches, mask, earlier_right_factors, left_u, panel_tiles,
    )
    solved, chol = panel(mesh, part, left, pivot_u, panel_tiles)
    chosen = jnp.logical_and(lax.axis_index("row") == owner_row, jnp.arange(slots) == local_slot)
    solved = solved.reshape(slots, TILE, -1)
    return jnp.where(chosen[:, None, None], chol[None], solved).reshape(panel_tiles.shape)


def solution(mesh):
    in_specs = (P("row", "col"), P("row", "col"), P("row", "col"), P())
    return jax.shard_map(
        functools.partial(local, mesh), mesh=mesh, in_specs=in_specs, out_specs=P("row", "col"), check_vma=False
    )
```

```python
import functools

import jax
import jax.numpy as jnp
from jax import lax
from jax.experimental import pallas as pl
from jax.experimental.pallas import tpu as pltpu
from jax.sharding import PartitionSpec as P

TILE = 1024
RANK = 256

BLK = 128
SUB = 8
FILL = 256
STRIP = 256
GROUP = 256
SKEW = 3
LAG = 2
F32 = jnp.float32
BF16 = jnp.bfloat16
HI = lax.Precision.HIGHEST
MESH = pl.DeviceIdType.MESH
ANY = pl.BlockSpec(memory_space=pl.ANY)
VM = pl.BlockSpec(memory_space=pltpu.VMEM)
TRANS = (((1,), (1,)), ((), ()))


def dot(a, b, dims=((1,), (0,))):
    return lax.dot_general(a, b, (dims, ((), ())), precision=HI, preferred_element_type=F32)


def window(start, size):
    return pl.ds(pl.multiple_of(start, size), size)


def remote(src, dst, send, recv, target):
    return pltpu.make_async_remote_copy(
        src_ref=src, dst_ref=dst, send_sem=send, recv_sem=recv, device_id=target, device_id_type=MESH
    )


def pick(table, index):
    value = jnp.int32(table[0])
    for i in range(1, len(table)):
        value = jnp.where(index == i, jnp.int32(table[i]), value)
    return value


def spread_kernel(
    owner, row_devices, pieces, mask_ref, v_ref, u_ref, a_ref, left_ref, pu_ref, part_ref,
    pv, v_own, u_own, a_own, pvt, pin, left_own, small, a_mine, a_got, sends, recvs, a_send, a_recv, local_sem,
):
    me = lax.axis_index("row")
    col = lax.axis_index("col")
    chips = row_devices // 2
    chip, core = me // 2, me % 2
    order = [i ^ (i >> 1) for i in range(chips)]
    if max(order) >= chips:
        order = list(range(chips))
    home = order.index(owner // 2)
    home_core = owner % 2
    place = pick([order.index(c) for c in range(chips)], chip)
    nexts = [pick(order, (place + chips + w) % chips) * 2 + core for w in (1, -1)]
    hops = [(chips + w * (place - home)) % chips for w in (1, -1)]
    pair = chip * 2 + 1 - core
    tile, width = pu_ref.shape
    half = tile // 2
    step = half // (2 * pieces)
    share = tile // row_devices
    rank = RANK
    blocks = width // rank
    slots = v_ref.shape[0] // tile

    loads = [
        pltpu.make_async_copy(src, dst, local_sem.at[i])
        for i, (src, dst) in enumerate(((v_ref, v_own), (u_ref, u_own), (a_ref, a_own)))
    ]
    loads[0].start()

    barrier = pltpu.get_barrier_semaphore()
    for d in range(1, row_devices):
        pl.semaphore_signal(barrier, inc=1, device_id=((me + d) % row_devices, col), device_id_type=MESH)
    pl.semaphore_wait(barrier, row_devices - 1)
    loads[0].wait()
    loads[1].start()
    loads[2].start()

    bufs = (pv, pu_ref)

    def move(kind, way, side, i, target, lane):
        at = window(way * half + (2 * i + side) * step, step)
        ref = bufs[kind].at[at, :]
        return remote(ref, ref, sends.at[kind, lane, way, i], recvs.at[kind, way, side, i], (target, col))

    is_owner = me == owner
    away = chip != owner // 2
    helper = jnp.logical_and(jnp.logical_not(away), jnp.logical_not(is_owner))

    def a_piece(target):
        return remote(a_mine.at[window(target * share, share), :], a_got, a_send.at[target], a_recv, (target, col))

    def chosen(src, dst):
        @pl.loop(0, tile // BLK)
        def _(n):
            total = None
            for t in range(slots):
                keep = mask_ref[t:t + 1, :dst.shape[1]].astype(dst.dtype)
                term = src[window(t * tile + n * BLK, BLK), :] * keep
                total = term if total is None else total + term
            dst[window(n * BLK, BLK), :] = total

    def first_sends(kind):
        @pl.loop(0, pieces)
        def _(i):
            for way in range(2):
                move(kind, way, 1 - home_core, i, owner ^ 1, 2).start()
                move(kind, way, home_core, i, nexts[way], 0).start()
            for way in range(2):
                move(kind, way, home_core, i, owner ^ 1, 1).start()

    @pl.when(is_owner)
    def _():
        chosen(v_own, pv)
        first_sends(0)
        loads[1].wait()
        chosen(u_own, pu_ref)
        first_sends(1)
        loads[2].wait()
        chosen(a_own, a_mine)
        for other in range(row_devices):
            if other != owner:
                a_piece(other).start()
        a_got[...] = a_mine[owner * share:(owner + 1) * share, :]

    @pl.when(jnp.logical_not(is_owner))
    def _():
        loads[1].wait()
        loads[2].wait()

    def relay(kind, tick):
        for way in range(2):
            i = tick - SKEW * jnp.maximum(hops[way] - 1, 0)

            @pl.when(jnp.logical_and(jnp.logical_not(is_owner), jnp.logical_and(i >= 0, i < pieces)))
            def _():
                move(kind, way, core, i, nexts[way], 0).wait_recv()

                @pl.when(hops[way] < chips - 1)
                def _():
                    move(kind, way, core, i, nexts[way], 0).start()

                @pl.when(away)
                def _():
                    move(kind, way, core, i, pair, 1).start()

    def gather(kind):
        @pl.when(jnp.logical_not(is_owner))
        def _():
            @pl.loop(0, pieces)
            def _(i):
                for way in range(2):
                    move(kind, way, 1 - core, i, pair, 1).wait_recv()

    ticks = pieces + SKEW * max(chips - 2, 0)

    @pl.loop(0, ticks)
    def _(tick):
        relay(0, tick)

    gather(0)
    each = max(1, ticks // (blocks * slots))
    during = min(ticks, each * blocks * slots)

    @pl.loop(0, blocks)
    def _(b):
        at = window(b * rank, rank)
        pvt[at, :] = pv[:, at].T
        pin[:, at] = jnp.dot(pvt[at, :], pv[:, at], preferred_element_type=F32).astype(BF16)

        @pl.loop(0, slots)
        def _(t):
            here = window(t * tile, tile)
            inner = jnp.dot(pvt[at, :], v_own[here, at], preferred_element_type=F32).astype(BF16)
            left_own[here, at] = lax.dot_general(
                u_own[here, at], inner, TRANS, preferred_element_type=F32
            ).astype(BF16)
            done = (b * slots + t) * each

            @pl.loop(jnp.minimum(done, during), jnp.minimum(done + each, during))
            def _(tick):
                relay(1, tick)

    left_out = pltpu.make_async_copy(left_own, left_ref, local_sem.at[3])
    left_out.start()

    @pl.loop(during, ticks)
    def _(tick):
        relay(1, tick)

    gather(1)
    rows = window(me * share, share)

    @pl.loop(0, blocks)
    def _(b):
        at = window(b * rank, rank)
        small[:, at] = lax.dot_general(
            pu_ref[rows, at], pin[:, at], TRANS, preferred_element_type=F32
        ).astype(BF16)

    @pl.loop(0, tile // rank)
    def _(n):
        at = window(n * rank, rank)
        part_ref[:, at] = -lax.dot_general(small[...], pu_ref[at, :], TRANS, preferred_element_type=F32)

    @pl.when(jnp.logical_not(is_owner))
    def _():
        a_piece(owner).wait_recv()

    mine_cols = window(col * a_got.shape[1], a_got.shape[1])
    part_ref[:, mine_cols] = part_ref[:, mine_cols] + a_got[...]
    left_out.wait()

    @pl.when(is_owner)
    def _():
        for kind in range(2):

            @pl.loop(0, pieces)
            def _(i):
                for way in range(2):
                    move(kind, way, home_core, i, nexts[way], 0).wait_send()
                    move(kind, way, home_core, i, owner ^ 1, 1).wait_send()
                    move(kind, way, 1 - home_core, i, owner ^ 1, 2).wait_send()

        for other in range(row_devices):
            if other != owner:
                a_piece(other).wait_send()

    @pl.when(jnp.logical_not(is_owner))
    def _():
        for kind in range(2):

            @pl.loop(0, pieces)
            def _(i):
                for way in range(2):

                    @pl.when(hops[way] < chips - 1)
                    def _():
                        move(kind, way, core, i, nexts[way], 0).wait_send()

                    @pl.when(away)
                    def _():
                        move(kind, way, core, i, pair, 1).wait_send()


def spread(mesh, owner, mask, v, u, tiles):
    row_devices = mesh.shape["row"]
    tile, width = TILE, v.shape[1]
    pieces = 8
    share = tile // row_devices
    return pl.pallas_call(
        functools.partial(spread_kernel, owner, row_devices, pieces),
        out_shape=(
            jax.ShapeDtypeStruct(u.shape, BF16),
            jax.ShapeDtypeStruct((tile, width), BF16),
            jax.ShapeDtypeStruct((share, tile), F32),
        ),
        in_specs=[VM, ANY, ANY, ANY],
        out_specs=(ANY, VM, VM),
        scratch_shapes=[
            pltpu.VMEM((tile, width), BF16),
            pltpu.VMEM(v.shape, BF16),
            pltpu.VMEM(u.shape, BF16),
            pltpu.VMEM(tiles.shape, F32),
            pltpu.VMEM((width, tile), BF16),
            pltpu.VMEM((RANK, width), BF16),
            pltpu.VMEM(u.shape, BF16),
            pltpu.VMEM((share, width), BF16),
            pltpu.VMEM((tile, tiles.shape[1]), F32),
            pltpu.VMEM((share, tiles.shape[1]), F32),
            pltpu.SemaphoreType.DMA((2, 3, 2, pieces)),
            pltpu.SemaphoreType.DMA((2, 2, 2, pieces)),
            pltpu.SemaphoreType.DMA((row_devices,)),
            pltpu.SemaphoreType.DMA,
            pltpu.SemaphoreType.DMA((4,)),
        ],
        compiler_params=pltpu.CompilerParams(
            collective_id=1 + owner, has_side_effects=True, vmem_limit_bytes=48 * 1024 * 1024
        ),
        cost_estimate=pl.CostEstimate(flops=20_000_000_000, bytes_accessed=30_000_000, transcendentals=0),
        name="spread",
    )(mask, v, u, tiles)


def eliminate(block):
    shape = (SUB, BLK)
    groups = [block[g * SUB:(g + 1) * SUB, :] for g in range(BLK // SUB)]
    lane = lax.broadcasted_iota(jnp.int32, shape, 1)
    sub = lax.broadcasted_iota(jnp.int32, shape, 0)
    for g in range(len(groups)):
        base = g * SUB
        rows = groups[g]
        cols = [jnp.broadcast_to(rows[:, base + j:base + j + 1], shape) for j in range(SUB)]
        out = rows
        for s in range(SUB):
            raw = jnp.broadcast_to(rows[s:s + 1, :], shape)
            here = lane == base + s
            mine = sub == s
            out = jnp.where(mine, raw, out)
            inverse = 1.0 / jnp.broadcast_to(cols[s][s:s + 1, :], shape)
            factor = jnp.where(mine, 0.0, cols[s] * inverse)
            unit = jnp.where(here, 1.0, raw)
            kept = jnp.where(here, 0.0, rows)
            rows = jnp.where(mine, unit * inverse, kept - factor * unit)
            for j in range(s + 1, SUB):
                head = jnp.broadcast_to(cols[j][s:s + 1, :], shape)
                cols[j] = jnp.where(mine, head * inverse, cols[j] - factor * head)
        groups[g] = out
        if g + 1 == len(groups):
            break
        reduced = [jnp.broadcast_to(rows[s:s + 1, :], shape) for s in range(SUB)]
        inside = jnp.logical_and(lane >= base, lane < base + SUB)
        for h in range(g + 1, len(groups)):
            old = groups[h]
            terms = [
                jnp.broadcast_to(old[:, base + s:base + s + 1], shape) * reduced[s] for s in range(SUB)
            ]
            while len(terms) > 1:
                terms = [terms[i] + terms[i + 1] for i in range(0, len(terms), 2)]
            groups[h] = jnp.where(inside, 0.0, old) - terms[0]
    return jnp.concatenate(groups, axis=0)


def factor_step(k, w_ref, l_ref, x_ref):
    size = w_ref.shape[0]
    count = size // BLK
    row_id = lax.broadcasted_iota(jnp.int32, (BLK, BLK), 0)
    col_id = lax.broadcasted_iota(jnp.int32, (BLK, BLK), 1)
    at = window(k * BLK, BLK)
    done = eliminate(w_ref[at, at])
    pivots = jnp.sum(jnp.where(row_id == col_id, done, 0.0), axis=1, keepdims=True)
    scale = 1.0 / jnp.sqrt(pivots)
    upper = jnp.where(col_id >= row_id, done * scale, 0.0)
    inner = jnp.where(col_id < row_id, done * scale, 0.0) + jnp.where(row_id == col_id, scale, 0.0)
    l_ref[at, at] = upper.T
    row = dot(inner, w_ref[at, :])
    block_id = lax.broadcasted_iota(jnp.int32, (BLK, size), 1) // BLK
    row = jnp.where(block_id == k, jnp.concatenate([inner] * count, axis=1), row)
    x_ref[at, :] = jnp.where(block_id <= k, row, 0.0)
    inner_t = inner.T

    strip_row = lax.broadcasted_iota(jnp.int32, (STRIP, BLK), 0) // BLK
    per = STRIP // BLK

    @pl.loop((k + 1) // per, count // per)
    def _(i):
        there = window(i * STRIP, STRIP)
        below = strip_row + i * per > k
        old = w_ref[there, at]
        left = jnp.where(below, dot(old, inner_t), 0.0)
        l_ref[there, at] = jnp.where(below, left, l_ref[there, at])
        w_ref[there, at] = jnp.where(below, 0.0, old)
        w_ref[there, :] = w_ref[there, :] - dot(left, row)


def panel_kernel(
    depth, row_devices, pieces, chunks, part_ref, left_ref, u_ref, a_ref, out_ref, lcol_ref,
    w_ref, l_ref, x_ref, acc, come, got, left_own, local_sem,
    sends, recvs, pair_send, pair_recv, line_send, line_recv, out_send, out_recv,
):
    me = lax.axis_index("row")
    col = lax.axis_index("col")
    chips = row_devices // 2
    chip, core = me // 2, me % 2
    share = part_ref.shape[0]
    sub = share // depth
    pair = chip * 2 + 1 - core
    cols = [(col + d) % depth for d in range(1, depth)]
    peers = [((chip + d) % chips) * 2 + core for d in range(1, chips)]
    size = w_ref.shape[0]
    width = a_ref.shape[1]
    half = acc.shape[0] // 2
    piece = half // pieces
    count = size // BLK
    load = pltpu.make_async_copy(left_ref, left_own, local_sem)
    load.start()

    barrier = pltpu.get_barrier_semaphore()
    for other in cols:
        pl.semaphore_signal(barrier, inc=1, device_id=(me, other), device_id_type=MESH)
    for other in peers + [pair]:
        pl.semaphore_signal(barrier, inc=1, device_id=(other, col), device_id_type=MESH)
    pl.semaphore_wait(barrier, depth + chips - 1)

    def groups_of(holder):
        return ((holder + 1) * share - 1) // GROUP + 1

    def over(holder, act):
        @pl.loop(0, groups_of(holder))
        def _(g):
            act(g, window(g * GROUP, GROUP))

    mine = window(me * share + col * sub, sub)

    def first(d, g, at):
        return remote(
            part_ref.at[window(cols[d] * sub, sub), at], got.at[d, :, at], sends.at[d, g], recvs.at[d, g], (me, cols[d])
        )

    def second(d, g, at):
        n = depth - 1 + d
        ref = w_ref.at[mine, at]
        return remote(ref, ref, sends.at[n, g], recvs.at[n, g], (me, cols[d]))

    def third(d, holder, g, at):
        n = 2 * (depth - 1) + d
        ref = w_ref.at[window(holder * share, share), at]
        return remote(ref, ref, sends.at[n, g], recvs.at[n, g], (peers[d], col))

    def fourth(d, holder, g, at):
        ref = w_ref.at[window(holder * share, share), at]
        return remote(ref, ref, pair_send.at[d, g], pair_recv.at[d, g], (pair, col))

    holders = [((chip + chips - d) % chips) * 2 + core for d in range(chips)]
    others = [((chip + chips - d) % chips) * 2 + 1 - core for d in range(chips)]
    for d in range(depth - 1):
        over(me, lambda g, at: first(d, g, at).start())

    mine_cols = window(col * width, width)
    strips = half // FILL

    def fill(q):
        @pl.loop(0, 2)
        def _(way):
            at = window(way * half + q * FILL, FILL)
            acc[at, :] = -lax.dot_general(left_own[at, :], u_ref[...], TRANS, preferred_element_type=F32)
            acc[at, mine_cols] = acc[at, mine_cols] + a_ref[at, :]

    def line(way, i, target):
        at = window(way * half + i * piece, piece)
        return remote(acc.at[at, :], come.at[at, :], line_send.at[way, i], line_recv.at[way, i], (me, target))

    def pass_on(way, i, seat, target):
        @pl.when(jnp.logical_and(i >= 0, i < pieces))
        def _():
            at = window(way * half + i * piece, piece)

            @pl.when(seat > 0)
            def _():
                line(way, i, target).wait_recv()
                acc[at, :] = acc[at, :] + come[at, :]

            @pl.when(seat < depth - 1)
            def _():
                line(way, i, target).start()

    up = jnp.minimum(col + 1, depth - 1)
    down = jnp.maximum(col - 1, 0)
    seat_down = depth - 1 - col

    def line_step(tick):
        pass_on(0, tick - LAG * seat_down, seat_down, down)
        pass_on(1, tick - LAG * col, col, up)

    def line_steps(lo, hi):
        @pl.loop(lo, hi)
        def _(tick):
            line_step(tick)

    def sum_share():
        def act(g, at):
            total = part_ref[window(col * sub, sub), at]
            for d in range(depth - 1):
                first(d, g, at).wait_recv()
                total = total + got[d, :, at]
            w_ref[mine, at] = total
            for d in range(depth - 1):
                second(d, g, at).start()

        over(me, act)

    def to_peers():
        def act(g, at):
            for d in range(depth - 1):
                second(d, g, at).wait_recv()
            for d in range(chips - 1):
                third(d, me, g, at).start()
            fourth(0, me, g, at).start()

        over(me, act)

    def to_pair(d):
        def act(g, at):
            third(d - 1, holders[d], g, at).wait_recv()
            fourth(d, holders[d], g, at).start()

        over(holders[d], act)

    ticks = pieces + LAG * (depth - 1)
    load.wait()
    ready = max(6, strips)

    @pl.loop(0, ready)
    def _(tick):
        @pl.when(tick < strips)
        def _():
            fill(tick)

        @pl.when(tick == 0)
        def _():
            sum_share()

        line_step(tick)

        @pl.when(tick == 2)
        def _():
            to_peers()

        @pl.when(tick == 4)
        def _():
            for d in range(1, chips - 1):
                to_pair(d)

    to_pair(chips - 1)
    for d in range(chips):
        over(others[d], lambda g, at: fourth(d, others[d], g, at).wait_recv())
    for d in range(depth - 1):
        over(me, lambda g, at: first(d, g, at).wait_send())
        over(me, lambda g, at: second(d, g, at).wait_send())
    for d in range(chips - 1):
        over(me, lambda g, at: third(d, me, g, at).wait_send())
    for d in range(chips):
        over(holders[d], lambda g, at: fourth(d, holders[d], g, at).wait_send())

    @pl.loop(0, count)
    def _(i):
        at = window(i * BLK, BLK)
        l_ref[at, :] = jnp.zeros((BLK, size), F32)
        w_ref[at, at] = (w_ref[at, at] + w_ref[at, at].T) * 0.5

        @pl.loop(i + 1, count)
        def _(j):
            there = window(j * BLK, BLK)
            w_ref[at, there] = w_ref[there, at].T

    after = min(ticks, ready + count)

    @pl.loop(0, count)
    def _(k):
        line_steps(jnp.minimum(ready + k, after), jnp.minimum(ready + k + 1, after))
        factor_step(k, w_ref, l_ref, x_ref)

    chunk = half // chunks

    def deal(way, i, c):
        at = window(way * half + i * chunk, chunk)
        return remote(
            come.at[at, c * width:(c + 1) * width], out_ref.at[at, :],
            out_send.at[i, c], out_recv.at[way, i], (me, c),
        )

    ends = [(0, 0), (1, depth - 1)]
    at_end = jnp.logical_or(col == 0, col == depth - 1)
    own_way = jnp.where(col == 0, 0, 1)

    def reach(i):
        even = after + i * (ticks - after) // chunks
        need = i * (pieces // chunks) + LAG * (depth - 1)
        return jnp.minimum(ticks, jnp.maximum(even, jnp.where(i > 0, need, after)))

    @pl.loop(0, chunks)
    def _(i):
        line_steps(reach(i), reach(i + 1))

        for way, end in ends:

            @pl.when(col == end)
            def _():
                at = window(way * half + i * chunk, chunk)
                for c in sorted(range(depth), key=lambda c: -abs(c - end)):
                    upto = (c + 1) * width
                    value = dot(acc[at, :upto], x_ref[c * width:upto, :upto], ((1,), (1,)))
                    if c == end:
                        out_ref[at, :] = value
                    else:
                        come[at, c * width:upto] = value
                        deal(way, i, c).start()

    lcol_ref[...] = l_ref[:, mine_cols]

    for way, end in ends:

        @pl.when(col != end)
        def _():
            @pl.loop(0, chunks)
            def _(i):
                deal(way, i, 0).wait_recv()

    @pl.when(at_end)
    def _():
        @pl.loop(0, chunks)
        def _(i):
            for c in range(depth):

                @pl.when(col != c)
                def _():
                    deal(own_way, i, c).wait_send()

    @pl.when(col > 0)
    def _():
        @pl.loop(0, pieces)
        def _(i):
            line(0, i, down).wait_send()

    @pl.when(col < depth - 1)
    def _():
        @pl.loop(0, pieces)
        def _(i):
            line(1, i, up).wait_send()


def panel(mesh, part, left, pivot_u, tiles):
    row_devices, depth = mesh.shape["row"], mesh.shape["col"]
    chips = row_devices // 2
    share, size = part.shape
    rows, width = tiles.shape
    pieces = rows // 2 // 64
    chunks = rows // 2 // 128
    links = 2 * (depth - 1) + chips - 1
    return pl.pallas_call(
        functools.partial(panel_kernel, depth, row_devices, pieces, chunks),
        out_shape=(
            jax.ShapeDtypeStruct((rows, width), F32),
            jax.ShapeDtypeStruct((size, width), F32),
        ),
        in_specs=[VM, ANY, VM, VM],
        out_specs=(VM, VM),
        scratch_shapes=[
            pltpu.VMEM((size, size), F32),
            pltpu.VMEM((size, size), F32),
            pltpu.VMEM((size, size), F32),
            pltpu.VMEM((rows, size), F32),
            pltpu.VMEM((rows, size), F32),
            pltpu.VMEM((depth - 1, share // depth, size), F32),
            pltpu.VMEM(left.shape, BF16),
            pltpu.SemaphoreType.DMA,
            pltpu.SemaphoreType.DMA((links, size // GROUP)),
            pltpu.SemaphoreType.DMA((links, size // GROUP)),
            pltpu.SemaphoreType.DMA((chips, size // GROUP)),
            pltpu.SemaphoreType.DMA((chips, size // GROUP)),
            pltpu.SemaphoreType.DMA((2, pieces)),
            pltpu.SemaphoreType.DMA((2, pieces)),
            pltpu.SemaphoreType.DMA((chunks, depth)),
            pltpu.SemaphoreType.DMA((2, chunks)),
        ],
        compiler_params=pltpu.CompilerParams(
            collective_id=0, has_side_effects=True, vmem_limit_bytes=58 * 1024 * 1024
        ),
        cost_estimate=pl.CostEstimate(flops=60_000_000_000, bytes_accessed=30_000_000, transcendentals=0),
        name="panel",
    )(part, left, pivot_u, tiles)


def local(mesh, panel_tiles, left_u, earlier_right_factors, tile_global_index):
    row_devices = mesh.shape["row"]
    tile_count = tile_global_index.shape[0]
    slots = panel_tiles.shape[0] // TILE
    here = tile_global_index == 0
    position = jnp.arange(tile_count, dtype=jnp.int32)
    owner_row = jnp.sum(jnp.where(here, position // slots, 0))
    mask = jnp.logical_and(here[None, :], (position % slots)[None, :] == jnp.arange(slots)[:, None])
    mask = jnp.sum(mask.astype(F32), axis=1)
    local_slot = jnp.sum(jnp.where(here, position % slots, 0))
    mask = jnp.broadcast_to(mask[:, None], (slots, left_u.shape[1]))
    branches = [functools.partial(spread, mesh, owner) for owner in range(row_devices)]
    left, pivot_u, part = lax.switch(
        owner_row, branches, mask, earlier_right_factors, left_u, panel_tiles,
    )
    solved, chol = panel(mesh, part, left, pivot_u, panel_tiles)
    chosen = jnp.logical_and(lax.axis_index("row") == owner_row, jnp.arange(slots) == local_slot)
    solved = solved.reshape(slots, TILE, -1)
    return jnp.where(chosen[:, None, None], chol[None], solved).reshape(panel_tiles.shape)


def solution(mesh):
    in_specs = (P("row", "col"), P("row", "col"), P("row", "col"), P())
    return jax.shard_map(
        functools.partial(local, mesh), mesh=mesh, in_specs=in_specs, out_specs=P("row", "col"), check_vma=False
    )
```
